512 devices in a mesh: seq: 64 (over y, x, core), head: 8 (over z).
Axes of the slice: x: 4, y: 8, z: 8, core: 2. Of those that a mesh axis runs over, the one named last changes fastest.
Arguments:
- queries: bfloat16 [32768, 4096], P(('seq', 'head')), may hold values from -5 to 5
- new_keys: bfloat16 [32768, 1024], P(('seq', 'head')), may hold values from -12 to 12
- new_values: bfloat16 [32768, 1024], P(('seq', 'head')), may hold values from -6 to 6
- cache_keys: bfloat16 [131072, 1024], P('seq', 'head'), may hold values from -12 to 12
- cache_values: bfloat16 [131072, 1024], P('seq', 'head'), may hold values from -6 to 6
- tile_lists: int32 [256, 8, 12], P('seq', 'head'), may hold values from 0 to 1023, as said below
Outputs:
- attended: bfloat16 [32768, 4096], P(('seq', 'head'))
The draws below stay inside these ranges and needn't reach their ends.
Inputs may be any that keep to these rules, and one draw needn't show every extreme that they name: `tile_lists`: for one key head, the 12 tiles of one block's list are distinct; the lists of the 4 blocks of one index of seq together name exactly 24 distinct tiles, at most 2 of them of one index of seq (tiles k * 16 to k * 16 + 15), and some index has exactly 2.
All inputs are finite; a program needn't handle non-finite values.
Results may differ from the reference program's by a relative error of at most 0.003.
Values may be sent and summed in bfloat16 or wider, within the bound.
A program may use at most 64 MiB of HBM per device.

```python
import math
import jax
import jax.numpy as jnp
from jax import lax

HQ = 32
KV = 8
HD = 128
QB = 128
TILE = 128
SEL = 12
NQB_DEV = 4
TILES_DEV = 16
POOL = 24
CAP = 2
PROMPT = 32768
CTX = 131072
NQB = 256
N_SEQ = 64


def one_group(group_key):
    slot_count = N_SEQ * CAP
    owner_of = jnp.arange(slot_count) // CAP
    rank_of = jnp.arange(slot_count) % CAP
    order_key, force_key, offset_key, mix_key = jax.random.split(group_key, 4)
    shuffle = jax.random.permutation(order_key, slot_count)
    forced = jax.random.randint(force_key, (), 0, N_SEQ)
    slot_score = jnp.where(owner_of == forced, rank_of - CAP, shuffle)
    ordering = jnp.argsort(slot_score, stable=True)[:POOL]
    offsets = jax.random.randint(offset_key, (N_SEQ,), 0, TILES_DEV)
    picked_owner = owner_of[ordering]
    picked_rank = rank_of[ordering]
    pool_ids = picked_owner * TILES_DEV + (offsets[picked_owner] + picked_rank) % TILES_DEV
    pool_ids = pool_ids[jax.random.permutation(mix_key, POOL)]
    position = (jnp.arange(NQB_DEV)[:, None] * SEL + jnp.arange(SEL)[None, :]) % POOL
    return pool_ids[position].astype(jnp.int32)


def draw_tile_lists(key, part):
    group_keys = jax.random.split(key, N_SEQ * KV)
    grouped = jax.vmap(one_group)(group_keys).reshape(N_SEQ, KV, NQB_DEV, SEL)
    return jnp.transpose(grouped, (0, 2, 1, 3)).reshape(NQB, KV, SEL)


def draw_queries(key, part):
    values = jax.random.truncated_normal(jax.random.fold_in(key, 1), -5.0, 5.0, (PROMPT, HQ * HD))
    return values.astype(jnp.float32).astype(jnp.bfloat16)


def draw_new_keys(key, part):
    values = 2.5 * jax.random.truncated_normal(jax.random.fold_in(key, 2), -4.8, 4.8, (PROMPT, KV * HD))
    return values.astype(jnp.float32).astype(jnp.bfloat16)


def block_levels(key, shape, cuts, smallest, high):
    def one(axis_at, shards_of):
        heights = jax.random.uniform(jax.random.fold_in(jax.random.fold_in(key, 6), axis_at), (shards_of,), jnp.float32, smallest / len(cuts), high / len(cuts))
        return jnp.repeat(jnp.exp(heights), shape[axis_at] // shards_of).reshape((-1,) + (1,) * (len(shape) - axis_at - 1))

    level = one(*cuts[0])
    for cut in cuts[1:]:
        level = level * one(*cut)
    return level


def noise(own_key, extent, spread, limit, pieces=(), kind=jnp.bfloat16):
    values = jax.random.normal(own_key, extent, jnp.float32) * spread
    if len(pieces) > 0:
        values = block_levels(own_key, extent, pieces, -0.22, 0.18) * values
    return jnp.clip(values, min=-limit, max=limit).astype(kind)


def setup_inputs(seed: int = 0) -> dict:
    key_list = jax.random.split(jax.random.key(seed), 7)
    queries = draw_queries(jax.random.fold_in(key_list[6], 71), 0)
    new_keys = draw_new_keys(jax.random.fold_in(key_list[6], 71), 0)
    new_values = noise(key_list[2], (PROMPT, KV * HD), 1.0, 6.0, ((0, 512),))
    cache_keys = noise(key_list[3], (CTX, KV * HD), 2.5, 12.0, ((0, 64), (1, 8)))
    cache_values = noise(key_list[4], (CTX, KV * HD), 1.0, 6.0, ((0, 64), (1, 8)))
    tile_lists = draw_tile_lists(jax.random.fold_in(key_list[6], 71), 0)
    return dict(queries=queries, new_keys=new_keys, new_values=new_values, cache_keys=cache_keys, cache_values=cache_values, tile_lists=tile_lists)


NEG_FILL = -1e+30

def reference(queries, new_keys, new_values, cache_keys, cache_values, tile_lists):
    group_size = HQ // KV
    scale_factor = 1.0 / math.sqrt(HD)
    query_blocks = queries.reshape(NQB, QB, KV, group_size, HD)
    key_blocks = new_keys.reshape(NQB, QB, KV, HD)
    value_blocks = new_values.reshape(NQB, QB, KV, HD)
    key_tiles = cache_keys.reshape(CTX // TILE, TILE, KV, HD)
    value_tiles = cache_values.reshape(CTX // TILE, TILE, KV, HD)
    head_pick = jnp.arange(KV)[:, None]
    causal = jnp.arange(QB)[:, None] >= jnp.arange(QB)[None, :]

    def one_block(block_index):
        query_block = query_blocks[block_index].astype(jnp.float32)
        chosen = tile_lists[block_index]
        earlier = jnp.maximum(block_index - 1, 0)
        context_keys = key_tiles[chosen, :, head_pick].reshape(KV, SEL * TILE, HD)
        context_values = value_tiles[chosen, :, head_pick].reshape(KV, SEL * TILE, HD)
        all_keys = jnp.concatenate([context_keys, jnp.transpose(key_blocks[earlier], (1, 0, 2)), jnp.transpose(key_blocks[block_index], (1, 0, 2))], axis=1).astype(jnp.float32)
        all_values = jnp.concatenate([context_values, jnp.transpose(value_blocks[earlier], (1, 0, 2)), jnp.transpose(value_blocks[block_index], (1, 0, 2))], axis=1).astype(jnp.float32)
        scores = jnp.einsum('qhgd,hkd->hgqk', query_block, all_keys) * scale_factor
        has_prior = jnp.broadcast_to(block_index >= 1, (QB, QB))
        visible = jnp.concatenate([jnp.ones((QB, SEL * TILE), dtype=bool), has_prior, causal], axis=1)
        masked = jnp.where(visible, scores, NEG_FILL)
        row_top = lax.optimization_barrier(jnp.max(masked, axis=3, keepdims=True))
        exponent = jnp.exp(masked - row_top)
        row_total = lax.optimization_barrier(jnp.sum(exponent, axis=3))
        weights = lax.optimization_barrier(exponent.astype(jnp.bfloat16)).astype(jnp.float32)
        weighted = jnp.einsum('hgqk,hkd->qhgd', weights, all_values)
        result = weighted / jnp.transpose(row_total, (2, 0, 1))[..., None]
        return result.astype(jnp.bfloat16).reshape(QB, HQ * HD)
    return lax.map(one_block, jnp.arange(NQB)).reshape(PROMPT, HQ * HD)
```

```python
import functools
import math

import jax
import jax.numpy as jnp
from jax import lax
from jax.experimental import pallas as pl
from jax.experimental.pallas import tpu as pltpu
from jax.sharding import PartitionSpec as P

KV = 8
HD = 128
QB = 128
TILE = 128
SEL = 12
GROUP = 4

RING = 8
ROW = 8
HEADS = 8
HELD = 16
CHUNK = 4
CHUNKS = HELD // CHUNK
BLOCKS = 4
ROWS = BLOCKS * QB
PART = ROWS // HEADS
WIDE = GROUP * HD
REMOTE = SEL * TILE
KEYS = REMOTE + 2 * QB
NEG_FILL = -1e30
EXP2_SCALE = math.log2(math.e) / math.sqrt(HD)
MESH = pl.DeviceIdType.MESH
ORDER = (2, 1, 3, 0)
SOFT_ROWS = 32


def kernel(
    q_in, k_in, v_in, key_tiles, value_tiles, list_in, slots,
    out,
    q_rows, k_loc, v_loc, row_lists, table, table_smem,
    kb1, kb2, kb3, kb4, kb5, kb6, kb7,
    vb1, vb2, vb3, vb4, vb5, vb6, vb7,
    stage, got_k, got_v, stacked, gathered, scores, weights, totals, out_stage,
    list_send, list_recv, plan_sem, y_send, y_recv, x_send, x_recv,
    z_send, z_recv, z_local, prev_send, prev_recv, o_send, o_recv, o_local,
):
    seq = lax.axis_index("seq")
    z = lax.axis_index("head")
    y = seq // ROW
    col = seq % ROW
    ahead = (seq + ROW) % (RING * ROW)
    behind = (seq + (RING - 1) * ROW) % (RING * ROW)
    after = (seq + 1) % (RING * ROW)
    before = (seq + RING * ROW - 1) % (RING * ROW)
    blocks_of = ((key_tiles, kb1, kb2, kb3, kb4, kb5, kb6, kb7), (value_tiles, vb1, vb2, vb3, vb4, vb5, vb6, vb7))
    got = (got_k, got_v)

    def row_peer(o):
        return y * ROW + (col + o) % ROW

    def head_peer(o):
        return (z + o) % HEADS

    barrier = pltpu.get_barrier_semaphore()

    def greet(where):
        pl.semaphore_signal(barrier, inc=1, device_id=where, device_id_type=MESH)

    for o in range(1, ROW):
        greet((row_peer(o), z))
    for o in range(1, HEADS):
        greet((seq, head_peer(o)))
    greet((ahead, z))
    greet((behind, z))
    greet((before, HEADS - 2))
    greet((before, HEADS - 1))
    is_last = z >= HEADS - 2
    pl.semaphore_wait(barrier, ROW - 1 + HEADS - 1 + 2 + jnp.where(is_last, HEADS, 0))

    def remote(src, dst, send, recv, where):
        return pltpu.make_async_remote_copy(
            src_ref=src, dst_ref=dst, send_sem=send, recv_sem=recv, device_id=where, device_id_type=MESH
        )

    def list_copy(o):
        return remote(list_in, row_lists.at[col], list_send.at[o - 1], list_recv.at[o - 1], (row_peer(o), z))

    def ring_copy(kv, way, hop, chunk):
        refs = blocks_of[kv]
        if way == 0:
            src, dst, where = refs[hop - 1], refs[hop], ahead
        else:
            src, dst, where = refs[(RING - hop + 1) % RING], refs[RING - hop], behind
        part = pl.ds(chunk * CHUNK, CHUNK)
        return remote(
            src.at[part], dst.at[part], y_send.at[kv, way, hop - 1, chunk], y_recv.at[kv, way, hop - 1, chunk], (where, z)
        )

    def row_copy(kv, rel, o):
        return remote(
            stage.at[kv, rel, o - 1],
            got[kv].at[pl.ds(col * 2 * RING + 2 * rel, 2)],
            x_send.at[kv, rel, o - 1],
            x_recv.at[kv, rel, o - 1],
            (row_peer(o), z),
        )

    def head_copies(o):
        to = head_peer(o)
        wide = pl.ds(pl.multiple_of(to * WIDE, WIDE), WIDE)
        narrow = pl.ds(pl.multiple_of(to * HD, HD), HD)
        rows = pl.ds(pl.multiple_of(z * PART, PART), PART)
        new_rows = pl.ds(pl.multiple_of(QB + z * PART, PART), PART)
        triples = ((q_in.at[:, wide], q_rows.at[rows]), (k_in.at[:, narrow], k_loc.at[new_rows]), (v_in.at[:, narrow], v_loc.at[new_rows]))
        if o == 0:
            return [pltpu.make_async_copy(src, dst, z_local.at[i]) for i, (src, dst) in enumerate(triples)]
        return [
            remote(src, dst, z_send.at[i, o - 1], z_recv.at[i, o - 1], (seq, to)) for i, (src, dst) in enumerate(triples)
        ]

    def prior_copies(to):
        source = z % 2
        narrow = pl.ds(to * HD, HD)
        rows = pl.ds(pl.multiple_of(source * PART, PART), PART)
        return [
            remote(k_in.at[:, narrow], k_loc.at[rows], prev_send.at[0, to], prev_recv.at[0, source], (after, to)),
            remote(v_in.at[:, narrow], v_loc.at[rows], prev_send.at[1, to], prev_recv.at[1, source], (after, to)),
        ]

    def forward(kv, hop, chunks):
        for chunk in chunks:
            ring_copy(kv, 0, hop, chunk).start()
            ring_copy(kv, 1, hop, chunk).start()

    for o in range(1, ROW):
        list_copy(o).start()
    forward(0, 1, range(CHUNKS))
    for o in range(HEADS):
        for copy in head_copies(o):
            copy.start()

    @pl.when(is_last)
    def _():
        for to in range(HEADS):
            for copy in prior_copies(to):
                copy.start()

    for o in range(1, ROW):
        list_copy(o).wait()
    row_lists[col] = list_in[...]
    lane = lax.broadcasted_iota(jnp.int32, (ROW, 128), 1)
    device = lax.broadcasted_iota(jnp.int32, (ROW, 128), 0)
    listed = row_lists[0]
    for d in range(1, ROW):
        listed = jnp.where(device == d, row_lists[d], listed)
    plan = jnp.zeros((ROW, 128), jnp.int32)
    for rel in range(RING):
        owner = ((y + RING - rel) % RING) * ROW + col
        mine = lax.shift_right_arithmetic(listed, 4) == owner
        tile = jnp.bitwise_and(listed, HELD - 1)
        smallest = jnp.min(jnp.where(mine, tile, HELD - 1), axis=1, keepdims=True)
        largest = jnp.max(jnp.where(mine, tile, 0), axis=1, keepdims=True)
        plan = jnp.where(lane == 2 * rel, smallest, plan)
        plan = jnp.where(lane == 2 * rel + 1, largest, plan)
    table[...] = plan

    def pack(kv, rel):
        source = blocks_of[kv][rel]

        def one(o, carry):
            to = (col + o) % ROW
            for rank in range(2):
                pick = jnp.bitwise_and(table_smem[to, 2 * rel + rank], HELD - 1)
                stage[kv, rel, o - 1, rank] = source[pick]
            return carry

        lax.fori_loop(1, ROW, one, 0)
        for rank in range(2):
            pick = jnp.bitwise_and(table_smem[col, 2 * rel + rank], HELD - 1)
            got[kv][col * 2 * RING + 2 * rel + rank] = source[pick]

    def hand_out(kv, rel):
        for o in range(1, ROW):
            row_copy(kv, rel, o).start()

    def travel(kv, first):
        packed = []
        for hop in range(1, 4):
            for chunk in range(CHUNKS):
                for way in range(2):
                    ring_copy(kv, way, hop, chunk).wait_recv()
                    if hop < 3 or (chunk < CHUNKS // 2) == (way == 0):
                        ring_copy(kv, way, hop + 1, chunk).start()
                if hop == 1 and chunk == 0:
                    first()
                    pack(kv, 0)
                    packed.append(0)
                if chunk == 1:
                    for rel in packed:
                        hand_out(kv, rel)
                    packed = []
            pack(kv, hop)
            pack(kv, RING - hop)
            packed += [hop, RING - hop]
        return packed

    def arrive(kv):
        for chunk in range(CHUNKS // 2):
            ring_copy(kv, 0, 4, chunk).wait_recv()
            ring_copy(kv, 1, 4, CHUNKS // 2 + chunk).wait_recv()
        pack(kv, 4)

    def read_plan():
        copy = pltpu.make_async_copy(table, table_smem, plan_sem)
        copy.start()
        copy.wait()

    packed = travel(0, read_plan)
    forward(1, 1, range(CHUNKS))
    for rel in packed:
        hand_out(0, rel)
    arrive(0)
    hand_out(0, 4)

    packed = travel(1, lambda: None)
    for rel in packed:
        hand_out(1, rel)
    arrive(1)
    hand_out(1, 4)

    for copy in head_copies(0):
        copy.wait()
    for o in range(1, HEADS):
        for copy in head_copies(o):
            copy.wait()
    for source in range(2):
        rows = pl.ds(source * PART, PART)
        for kv, ref in enumerate((k_loc, v_loc)):
            pltpu.make_async_copy(ref.at[rows], ref.at[rows], prev_recv.at[kv, source]).wait()
    for rel in range(RING):
        for o in range(1, ROW):
            row_copy(0, rel, o).wait()

    def block_at(step):
        return (z // 2 + step) % BLOCKS

    def gather(source, block):
        def one(j, carry):
            pick = jnp.bitwise_and(slots[block * SEL + j], 2 * RING * ROW - 1)
            gathered[pl.ds(pl.multiple_of(j * TILE, TILE), TILE), :] = source[pick]
            return carry

        lax.fori_loop(0, SEL, one, 0)

    def score(step, carry):
        block = block_at(step)
        first_row = pl.multiple_of(block * QB, QB)
        gather(got_k, block)
        for h in range(GROUP):
            stacked[pl.ds(h * QB, QB), :] = q_rows[pl.ds(first_row, QB), pl.ds(h * HD, HD)]
        contract = (((1,), (1,)), ((), ()))
        gathered[pl.ds(REMOTE, 2 * QB), :] = k_loc[pl.ds(first_row, 2 * QB), :]
        for pair in range(KEYS // (2 * TILE)):
            part = pl.ds(pair * 2 * TILE, 2 * TILE)
            scores[:, part] = lax.dot_general(stacked[...], gathered[part, :], contract, preferred_element_type=jnp.float32)
        from_column = jnp.where(block + seq > 0, 0, QB)
        row = lax.broadcasted_iota(jnp.int32, (SOFT_ROWS, 2 * QB), 0)
        column = lax.broadcasted_iota(jnp.int32, (SOFT_ROWS, 2 * QB), 1)

        def soften(i, inner):
            first = pl.multiple_of(i * SOFT_ROWS, SOFT_ROWS)
            rows = pl.ds(first, SOFT_ROWS)
            visible = (column - QB <= row + first % QB) & (column >= from_column)
            far = scores[rows, pl.ds(0, REMOTE)]
            near = jnp.where(visible, scores[rows, pl.ds(REMOTE, 2 * QB)], NEG_FILL)
            top = jnp.maximum(jnp.max(far, axis=1, keepdims=True), jnp.max(near, axis=1, keepdims=True))
            far = jnp.exp2((far - top) * EXP2_SCALE)
            near = jnp.exp2((near - top) * EXP2_SCALE)
            total = jnp.sum(far, axis=1, keepdims=True) + jnp.sum(near, axis=1, keepdims=True)
            weights[step, rows, pl.ds(0, REMOTE)] = far.astype(jnp.bfloat16)
            weights[step, rows, pl.ds(REMOTE, 2 * QB)] = near.astype(jnp.bfloat16)
            totals[step, rows, :] = jnp.broadcast_to(total, (SOFT_ROWS, HD))
            return inner

        return lax.fori_loop(0, GROUP * QB // SOFT_ROWS, soften, carry)

    lax.fori_loop(0, BLOCKS, score, 0)

    for rel in range(RING):
        for o in range(1, ROW):
            row_copy(1, rel, o).wait()

    def out_copy(to, place):
        rows = pl.ds(pl.multiple_of(to * PART, PART), PART)
        wide = pl.ds(pl.multiple_of(z * WIDE, WIDE), WIDE)
        return out_stage.at[rows], out.at[:, wide], place, to

    def attend(step):
        block = block_at(step)
        first_row = pl.multiple_of(block * QB, QB)
        gather(got_v, block)
        gathered[pl.ds(REMOTE, 2 * QB), :] = v_loc[pl.ds(first_row, 2 * QB), :]
        total = jnp.dot(weights[step], gathered[...], preferred_element_type=jnp.float32)
        result = (total / totals[step]).astype(jnp.bfloat16)
        for h in range(GROUP):
            out_stage[pl.ds(first_row, QB), pl.ds(h * HD, HD)] = result[h * QB : (h + 1) * QB]

    returns = []
    for step in ORDER:
        attend(step)
        if step != 0:
            for half in range(2):
                to = 2 * block_at(step) + half
                place = 2 * step + (z + half) % 2
                copy = out_copy(to, place)
                returns.append(remote(copy[0], copy[1], o_send.at[place], o_recv.at[place], (seq, to)))
                returns[-1].start()
        else:
            to = z + 1 - 2 * (z % 2)
            copy = out_copy(to, 0)
            returns.append(remote(copy[0], copy[1], o_send.at[0], o_recv.at[0], (seq, to)))
            returns[-1].start()
            own = out_copy(z, 0)
            local = pltpu.make_async_copy(own[0], own[1], o_local)
            local.start()
    local.wait()
    for copy in returns:
        copy.wait()

    for kv in range(2):
        for hop in range(1, 5):
            for chunk in range(CHUNKS):
                for way in range(2):
                    if hop < 4 or (chunk < CHUNKS // 2) == (way == 0):
                        ring_copy(kv, way, hop, chunk).wait_send()

    @pl.when(is_last)
    def _():
        for to in range(HEADS):
            for copy in prior_copies(to):
                copy.wait_send()


def on_device(queries, new_keys, new_values, cache_keys, cache_values, tile_lists):
    y = lax.axis_index("seq") // ROW
    listed = tile_lists.reshape(BLOCKS * SEL)
    list_in = jnp.broadcast_to(
        jnp.pad(listed, (0, 128 - BLOCKS * SEL), constant_values=-1)[None, :], (8, 128)
    )
    owner = listed // HELD
    not_smallest = jnp.any((owner[:, None] == owner[None, :]) & (listed[None, :] < listed[:, None]), axis=1)
    rel = (y - owner // ROW) % RING
    slots = ((owner % ROW) * RING + rel) * 2 + not_smallest.astype(jnp.int32)

    tiles = pltpu.VMEM((HELD, TILE, HD), jnp.bfloat16)
    dma = pltpu.SemaphoreType.DMA
    vmem = pl.BlockSpec(memory_space=pltpu.VMEM)
    return pl.pallas_call(
        kernel,
        out_shape=jax.ShapeDtypeStruct((PART, HEADS * WIDE), jnp.bfloat16),
        in_specs=[vmem] * 6 + [pl.BlockSpec(memory_space=pltpu.SMEM)],
        out_specs=vmem,
        scratch_shapes=[
            pltpu.VMEM((ROWS, WIDE), jnp.bfloat16),
            pltpu.VMEM((QB + ROWS, HD), jnp.bfloat16),
            pltpu.VMEM((QB + ROWS, HD), jnp.bfloat16),
            pltpu.VMEM((ROW, 8, 128), jnp.int32),
            pltpu.VMEM((ROW, 128), jnp.int32),
            pltpu.SMEM((ROW, 128), jnp.int32),
            *([tiles] * 14),
            pltpu.VMEM((2, RING, ROW - 1, 2, TILE, HD), jnp.bfloat16),
            pltpu.VMEM((2 * RING * ROW, TILE, HD), jnp.bfloat16),
            pltpu.VMEM((2 * RING * ROW, TILE, HD), jnp.bfloat16),
            pltpu.VMEM((GROUP * QB, HD), jnp.bfloat16),
            pltpu.VMEM((KEYS, HD), jnp.bfloat16),
            pltpu.VMEM((GROUP * QB, KEYS), jnp.float32),
            pltpu.VMEM((BLOCKS, GROUP * QB, KEYS), jnp.bfloat16),
            pltpu.VMEM((BLOCKS, GROUP * QB, HD), jnp.float32),
            pltpu.VMEM((ROWS, WIDE), jnp.bfloat16),
            dma((ROW - 1,)),
            dma((ROW - 1,)),
            dma,
            dma((2, 2, 4, CHUNKS)),
            dma((2, 2, 4, CHUNKS)),
            dma((2, RING, ROW - 1)),
            dma((2, RING, ROW - 1)),
            dma((3, HEADS - 1)),
            dma((3, HEADS - 1)),
            dma((3,)),
            dma((2, HEADS)),
            dma((2, 2)),
            dma((HEADS,)),
            dma((HEADS,)),
            dma,
        ],
        compiler_params=pltpu.CompilerParams(
            collective_id=0, has_side_effects=True, vmem_limit_bytes=64000 * 1024
        ),
    )(
        queries,
        new_keys,
        new_values,
        cache_keys.reshape(HELD, TILE, HD),
        cache_values.reshape(HELD, TILE, HD),
        list_in,
        slots,
    )


def solution(mesh):
    return jax.shard_map(
        on_device,
        mesh=mesh,
        in_specs=(
            P(("seq", "head"), None),
            P(("seq", "head"), None),
            P(("seq", "head"), None),
            P("seq", "head"),
            P("seq", "head"),
            P("seq", "head", None),
        ),
        out_specs=P(("seq", "head"), None),
        check_vma=False,
    )
```

```python
import functools
import math

import jax
import jax.numpy as jnp
from jax import lax
from jax.experimental import pallas as pl
from jax.experimental.pallas import tpu as pltpu
from jax.sharding import PartitionSpec as P

KV = 8
HD = 128
QB = 128
TILE = 128
SEL = 12
GROUP = 4

RING = 8
ROW = 8
HEADS = 8
HELD = 16
CHUNK = 4
CHUNKS = HELD // CHUNK
BLOCKS = 4
ROWS = BLOCKS * QB
PART = ROWS // HEADS
WIDE = GROUP * HD
REMOTE = SEL * TILE
KEYS = REMOTE + 2 * QB
NEG_FILL = -1e30
EXP2_SCALE = math.log2(math.e) / math.sqrt(HD)
MESH = pl.DeviceIdType.MESH
ORDER = (2, 1, 3, 0)
SOFT_ROWS = 32


def kernel(
    q_in, k_in, v_in, key_tiles, value_tiles, lists,
    out,
    q_rows, k_loc, v_loc, list_raw, list_in, row_lists, table, table_smem, slot_table, slots,
    kb1, kb2, kb3, kb4, kb5, kb6, kb7,
    vb1, vb2, vb3, vb4, vb5, vb6, vb7,
    stage, got_k, got_v, stacked, gathered, scores, weights, totals, out_stage,
    list_send, list_recv, plan_sem, slot_sem, y_send, y_recv, x_send, x_recv,
    z_send, z_recv, z_local, prev_send, prev_recv, o_send, o_recv, o_local,
):
    seq = lax.axis_index("seq")
    z = lax.axis_index("head")
    y = seq // ROW
    col = seq % ROW
    ahead = (seq + ROW) % (RING * ROW)
    behind = (seq + (RING - 1) * ROW) % (RING * ROW)
    after = (seq + 1) % (RING * ROW)
    before = (seq + RING * ROW - 1) % (RING * ROW)
    blocks_of = ((key_tiles, kb1, kb2, kb3, kb4, kb5, kb6, kb7), (value_tiles, vb1, vb2, vb3, vb4, vb5, vb6, vb7))
    got = (got_k, got_v)

    def row_peer(o):
        return y * ROW + (col + o) % ROW

    def head_peer(o):
        return (z + o) % HEADS

    lane = lax.broadcasted_iota(jnp.int32, (ROW, 128), 1)
    device = lax.broadcasted_iota(jnp.int32, (ROW, 128), 0)
    list_raw[...] = jnp.full((8, 128), -1, jnp.int32)
    for block in range(BLOCKS):
        list_raw[pl.ds(block, 1), pl.ds(0, SEL)] = lists[block]
    raw = list_raw[...]
    flat = jnp.full((8, 128), -1, jnp.int32)
    for block in range(BLOCKS):
        moved = pltpu.roll(jnp.broadcast_to(raw[block : block + 1], (8, 128)), block * SEL, 1)
        flat = jnp.where((lane >= block * SEL) & (lane < (block + 1) * SEL), moved, flat)
    list_in[...] = flat

    barrier = pltpu.get_barrier_semaphore()

    def greet(where):
        pl.semaphore_signal(barrier, inc=1, device_id=where, device_id_type=MESH)

    for o in range(1, ROW):
        greet((row_peer(o), z))
    for o in range(1, HEADS):
        greet((seq, head_peer(o)))
    greet((ahead, z))
    greet((behind, z))
    greet((before, HEADS - 2))
    greet((before, HEADS - 1))
    is_last = z >= HEADS - 2
    pl.semaphore_wait(barrier, ROW - 1 + HEADS - 1 + 2 + jnp.where(is_last, HEADS, 0))

    def remote(src, dst, send, recv, where):
        return pltpu.make_async_remote_copy(
            src_ref=src, dst_ref=dst, send_sem=send, recv_sem=recv, device_id=where, device_id_type=MESH
        )

    def list_copy(o):
        return remote(list_in, row_lists.at[col], list_send.at[o - 1], list_recv.at[o - 1], (row_peer(o), z))

    def ring_copy(kv, way, hop, chunk):
        refs = blocks_of[kv]
        if way == 0:
            src, dst, where = refs[hop - 1], refs[hop], ahead
        else:
            src, dst, where = refs[(RING - hop + 1) % RING], refs[RING - hop], behind
        part = pl.ds(chunk * CHUNK, CHUNK)
        return remote(
            src.at[part], dst.at[part], y_send.at[kv, way, hop - 1, chunk], y_recv.at[kv, way, hop - 1, chunk], (where, z)
        )

    def row_copy(kv, rel, o):
        return remote(
            stage.at[kv, rel, o - 1],
            got[kv].at[pl.ds(col * 2 * RING + 2 * rel, 2)],
            x_send.at[kv, rel, o - 1],
            x_recv.at[kv, rel, o - 1],
            (row_peer(o), z),
        )

    def head_copies(o):
        to = head_peer(o)
        wide = pl.ds(pl.multiple_of(to * WIDE, WIDE), WIDE)
        narrow = pl.ds(pl.multiple_of(to * HD, HD), HD)
        rows = pl.ds(pl.multiple_of(z * PART, PART), PART)
        new_rows = pl.ds(pl.multiple_of(QB + z * PART, PART), PART)
        triples = ((q_in.at[:, wide], q_rows.at[rows]), (k_in.at[:, narrow], k_loc.at[new_rows]), (v_in.at[:, narrow], v_loc.at[new_rows]))
        if o == 0:
            return [pltpu.make_async_copy(src, dst, z_local.at[i]) for i, (src, dst) in enumerate(triples)]
        return [
            remote(src, dst, z_send.at[i, o - 1], z_recv.at[i, o - 1], (seq, to)) for i, (src, dst) in enumerate(triples)
        ]

    def prior_copies(to):
        source = z % 2
        narrow = pl.ds(to * HD, HD)
        rows = pl.ds(pl.multiple_of(source * PART, PART), PART)
        return [
            remote(k_in.at[:, narrow], k_loc.at[rows], prev_send.at[0, to], prev_recv.at[0, source], (after, to)),
            remote(v_in.at[:, narrow], v_loc.at[rows], prev_send.at[1, to], prev_recv.at[1, source], (after, to)),
        ]

    def forward(kv, hop, chunks):
        for chunk in chunks:
            ring_copy(kv, 0, hop, chunk).start()
            ring_copy(kv, 1, hop, chunk).start()

    for o in range(1, ROW):
        list_copy(o).start()
    forward(0, 1, range(CHUNKS))
    for o in range(HEADS):
        for copy in head_copies(o):
            copy.start()

    @pl.when(is_last)
    def _():
        for to in range(HEADS):
            for copy in prior_copies(to):
                copy.start()

    for o in range(1, ROW):
        list_copy(o).wait()
    row_lists[col] = list_in[...]
    listed = row_lists[0]
    for d in range(1, ROW):
        listed = jnp.where(device == d, row_lists[d], listed)
    plan = jnp.zeros((ROW, 128), jnp.int32)
    for rel in range(RING):
        owner = ((y + RING - rel) % RING) * ROW + col
        mine = lax.shift_right_arithmetic(listed, 4) == owner
        tile = jnp.bitwise_and(listed, HELD - 1)
        smallest = jnp.min(jnp.where(mine, tile, HELD - 1), axis=1, keepdims=True)
        largest = jnp.max(jnp.where(mine, tile, 0), axis=1, keepdims=True)
        plan = jnp.where(lane == 2 * rel, smallest, plan)
        plan = jnp.where(lane == 2 * rel + 1, largest, plan)
    table[...] = plan

    entries = BLOCKS * SEL
    across = jnp.broadcast_to(flat[0:1], (entries, 128))
    lanes = lax.broadcasted_iota(jnp.int32, (entries, 128), 1)
    diagonal = lanes == lax.broadcasted_iota(jnp.int32, (entries, 128), 0)
    down = jnp.max(jnp.where(diagonal, across, 0), axis=1, keepdims=True)
    owner = lax.shift_right_arithmetic(down, 4)
    earlier = (lax.shift_right_arithmetic(across, 4) == owner) & (across < down)
    rank = jnp.max(jnp.where(earlier, 1, 0), axis=1, keepdims=True)
    rel = jnp.bitwise_and(y - lax.shift_right_arithmetic(owner, 3), RING - 1)
    slot = (jnp.bitwise_and(owner, ROW - 1) * RING + rel) * 2 + rank
    slot_table[...] = jnp.broadcast_to(slot, (entries, 128))

    def pack(kv, rel):
        source = blocks_of[kv][rel]

        def one(o, carry):
            to = (col + o) % ROW
            for rank in range(2):
                pick = jnp.bitwise_and(table_smem[to, 2 * rel + rank], HELD - 1)
                stage[kv, rel, o - 1, rank] = source[pick]
            return carry

        lax.fori_loop(1, ROW, one, 0)
        for rank in range(2):
            pick = jnp.bitwise_and(table_smem[col, 2 * rel + rank], HELD - 1)
            got[kv][col * 2 * RING + 2 * rel + rank] = source[pick]

    def hand_out(kv, rel):
        for o in range(1, ROW):
            row_copy(kv, rel, o).start()

    def travel(kv, first, packed):
        for hop in range(1, 4):
            for chunk in range(CHUNKS):
                for way in range(2):
                    ring_copy(kv, way, hop, chunk).wait_recv()
                    if hop < 3 or (chunk < CHUNKS // 2) == (way == 0):
                        ring_copy(kv, way, hop + 1, chunk).start()
                if hop == 1 and chunk == 0:
                    first()
                if chunk == (1 if hop == 1 else 0):
                    for ready in packed:
                        hand_out(*ready)
                    packed = []
            pack(kv, hop)
            pack(kv, RING - hop)
            hand_out(kv, hop)
            packed.append((kv, RING - hop))
        return packed

    def arrive(kv):
        for chunk in range(CHUNKS // 2):
            ring_copy(kv, 0, 4, chunk).wait_recv()
            ring_copy(kv, 1, 4, CHUNKS // 2 + chunk).wait_recv()
        pack(kv, 4)

    def read_plan():
        copy = pltpu.make_async_copy(table, table_smem, plan_sem)
        copy.start()
        copy.wait()
        for kv in range(2):
            pack(kv, 0)
        hand_out(0, 0)

    packed = travel(0, read_plan, [(1, 0)])
    copy = pltpu.make_async_copy(slot_table, slots, slot_sem)
    copy.start()
    copy.wait()
    forward(1, 1, range(CHUNKS))
    for ready in packed:
        hand_out(*ready)
    arrive(0)
    hand_out(0, 4)

    packed = travel(1, lambda: None, [])
    for ready in packed:
        hand_out(*ready)
    arrive(1)
    hand_out(1, 4)

    for copy in head_copies(0):
        copy.wait()
    for o in range(1, HEADS):
        for copy in head_copies(o):
            copy.wait()
    for source in range(2):
        rows = pl.ds(source * PART, PART)
        for kv, ref in enumerate((k_loc, v_loc)):
            pltpu.make_async_copy(ref.at[rows], ref.at[rows], prev_recv.at[kv, source]).wait()
    for rel in range(RING):
        for o in range(1, ROW):
            row_copy(0, rel, o).wait()

    def block_at(step):
        return (z // 2 + step) % BLOCKS

    def gather(source, block):
        def one(j, carry):
            pick = jnp.bitwise_and(slots[block * SEL + j, 0], 2 * RING * ROW - 1)
            gathered[pl.ds(pl.multiple_of(j * TILE, TILE), TILE), :] = source[pick]
            return carry

        lax.fori_loop(0, SEL, one, 0)

    def score(step, carry):
        block = block_at(step)
        first_row = pl.multiple_of(block * QB, QB)
        gather(got_k, block)
        for h in range(GROUP):
            stacked[pl.ds(h * QB, QB), :] = q_rows[pl.ds(first_row, QB), pl.ds(h * HD, HD)]
        contract = (((1,), (1,)), ((), ()))
        gathered[pl.ds(REMOTE, 2 * QB), :] = k_loc[pl.ds(first_row, 2 * QB), :]
        for pair in range(KEYS // (2 * TILE)):
            part = pl.ds(pair * 2 * TILE, 2 * TILE)
            scores[:, part] = lax.dot_general(stacked[...], gathered[part, :], contract, preferred_element_type=jnp.float32)
        from_column = jnp.where(block + seq > 0, 0, QB)
        row = lax.broadcasted_iota(jnp.int32, (SOFT_ROWS, 2 * QB), 0)
        column = lax.broadcasted_iota(jnp.int32, (SOFT_ROWS, 2 * QB), 1)

        def soften(i, inner):
            first = pl.multiple_of(i * SOFT_ROWS, SOFT_ROWS)
            rows = pl.ds(first, SOFT_ROWS)
            visible = (column - QB <= row + first % QB) & (column >= from_column)
            far = scores[rows, pl.ds(0, REMOTE)]
            near = jnp.where(visible, scores[rows, pl.ds(REMOTE, 2 * QB)], NEG_FILL)
            top = jnp.maximum(jnp.max(far, axis=1, keepdims=True), jnp.max(near, axis=1, keepdims=True))
            far = jnp.exp2((far - top) * EXP2_SCALE)
            near = jnp.exp2((near - top) * EXP2_SCALE)
            total = jnp.sum(far, axis=1, keepdims=True) + jnp.sum(near, axis=1, keepdims=True)
            weights[step, rows, pl.ds(0, REMOTE)] = far.astype(jnp.bfloat16)
            weights[step, rows, pl.ds(REMOTE, 2 * QB)] = near.astype(jnp.bfloat16)
            totals[step, rows, :] = jnp.broadcast_to(total, (SOFT_ROWS, HD))
            return inner

        return lax.fori_loop(0, GROUP * QB // SOFT_ROWS, soften, carry)

    lax.fori_loop(0, BLOCKS, score, 0)

    for rel in range(RING):
        for o in range(1, ROW):
            row_copy(1, rel, o).wait()

    def out_copy(to, place):
        rows = pl.ds(pl.multiple_of(to * PART, PART), PART)
        wide = pl.ds(pl.multiple_of(z * WIDE, WIDE), WIDE)
        return out_stage.at[rows], out.at[:, wide], place, to

    def attend(step):
        block = block_at(step)
        first_row = pl.multiple_of(block * QB, QB)
        gather(got_v, block)
        gathered[pl.ds(REMOTE, 2 * QB), :] = v_loc[pl.ds(first_row, 2 * QB), :]
        total = jnp.dot(weights[step], gathered[...], preferred_element_type=jnp.float32)
        result = (total / totals[step]).astype(jnp.bfloat16)
        for h in range(GROUP):
            out_stage[pl.ds(first_row, QB), pl.ds(h * HD, HD)] = result[h * QB : (h + 1) * QB]

    returns = []
    for step in ORDER:
        attend(step)
        if step != 0:
            for half in range(2):
                to = 2 * block_at(step) + half
                place = 2 * step + (z + half) % 2
                copy = out_copy(to, place)
                returns.append(remote(copy[0], copy[1], o_send.at[place], o_recv.at[place], (seq, to)))
                returns[-1].start()
        else:
            to = z + 1 - 2 * (z % 2)
            copy = out_copy(to, 0)
            returns.append(remote(copy[0], copy[1], o_send.at[0], o_recv.at[0], (seq, to)))
            returns[-1].start()
            own = out_copy(z, 0)
            local = pltpu.make_async_copy(own[0], own[1], o_local)
            local.start()
    local.wait()
    for copy in returns:
        copy.wait()

    for kv in range(2):
        for hop in range(1, 5):
            for chunk in range(CHUNKS):
                for way in range(2):
                    if hop < 4 or (chunk < CHUNKS // 2) == (way == 0):
                        ring_copy(kv, way, hop, chunk).wait_send()

    @pl.when(is_last)
    def _():
        for to in range(HEADS):
            for copy in prior_copies(to):
                copy.wait_send()


def on_device(queries, new_keys, new_values, cache_keys, cache_values, tile_lists):
    tiles = pltpu.VMEM((HELD, TILE, HD), jnp.bfloat16)
    dma = pltpu.SemaphoreType.DMA
    vmem = pl.BlockSpec(memory_space=pltpu.VMEM)
    return pl.pallas_call(
        kernel,
        out_shape=jax.ShapeDtypeStruct((PART, HEADS * WIDE), jnp.bfloat16),
        in_specs=[vmem] * 6,
        out_specs=vmem,
        scratch_shapes=[
            pltpu.VMEM((ROWS, WIDE), jnp.bfloat16),
            pltpu.VMEM((QB + ROWS, HD), jnp.bfloat16),
            pltpu.VMEM((QB + ROWS, HD), jnp.bfloat16),
            pltpu.VMEM((8, 128), jnp.int32),
            pltpu.VMEM((8, 128), jnp.int32),
            pltpu.VMEM((ROW, 8, 128), jnp.int32),
            pltpu.VMEM((ROW, 128), jnp.int32),
            pltpu.SMEM((ROW, 128), jnp.int32),
            pltpu.VMEM((BLOCKS * SEL, 128), jnp.int32),
            pltpu.SMEM((BLOCKS * SEL, 128), jnp.int32),
            *([tiles] * 14),
            pltpu.VMEM((2, RING, ROW - 1, 2, TILE, HD), jnp.bfloat16),
            pltpu.VMEM((2 * RING * ROW, TILE, HD), jnp.bfloat16),
            pltpu.VMEM((2 * RING * ROW, TILE, HD), jnp.bfloat16),
            pltpu.VMEM((GROUP * QB, HD), jnp.bfloat16),
            pltpu.VMEM((KEYS, HD), jnp.bfloat16),
            pltpu.VMEM((GROUP * QB, KEYS), jnp.float32),
            pltpu.VMEM((BLOCKS, GROUP * QB, KEYS), jnp.bfloat16),
            pltpu.VMEM((BLOCKS, GROUP * QB, HD), jnp.float32),
            pltpu.VMEM((ROWS, WIDE), jnp.bfloat16),
            dma((ROW - 1,)),
            dma((ROW - 1,)),
            dma,
            dma,
            dma((2, 2, 4, CHUNKS)),
            dma((2, 2, 4, CHUNKS)),
            dma((2, RING, ROW - 1)),
            dma((2, RING, ROW - 1)),
            dma((3, HEADS - 1)),
            dma((3, HEADS - 1)),
            dma((3,)),
            dma((2, HEADS)),
            dma((2, 2)),
            dma((HEADS,)),
            dma((HEADS,)),
            dma,
        ],
        compiler_params=pltpu.CompilerParams(
            collective_id=0, has_side_effects=True, vmem_limit_bytes=64000 * 1024
        ),
    )(
        queries,
        new_keys,
        new_values,
        cache_keys.reshape(HELD, TILE, HD),
        cache_values.reshape(HELD, TILE, HD),
        tile_lists,
    )


def solution(mesh):
    return jax.shard_map(
        on_device,
        mesh=mesh,
        in_specs=(
            P(("seq", "head"), None),
            P(("seq", "head"), None),
            P(("seq", "head"), None),
            P("seq", "head"),
            P("seq", "head"),
            P("seq", "head", None),
        ),
        out_specs=P(("seq", "head"), None),
        check_vma=False,
    )
```

```python
import functools
import math

import jax
import jax.numpy as jnp
from jax import lax
from jax.experimental import pallas as pl
from jax.experimental.pallas import tpu as pltpu
from jax.sharding import PartitionSpec as P

KV = 8
HD = 128
QB = 128
TILE = 128
SEL = 12
GROUP = 4

RING = 8
ROW = 8
HEADS = 8
HELD = 16
CHUNK = 4
CHUNKS = HELD // CHUNK
BLOCKS = 4
ROWS = BLOCKS * QB
PART = ROWS // HEADS
WIDE = GROUP * HD
HALF = HD // 2
REMOTE = SEL * TILE
KEYS = REMOTE + 2 * QB
NEG_FILL = -1e30
EXP2_SCALE = math.log2(math.e) / math.sqrt(HD)
MESH = pl.DeviceIdType.MESH
ORDER = (2, 1, 3, 0)
SOFT_ROWS = 32


def kernel(
    q_hbm, k_hbm, v_hbm, keys_hbm, values_hbm, lists,
    out,
    q_in, k_in, v_in, key_tiles, value_tiles, q_rows, k_loc, v_loc, list_raw, list_in, row_lists, table, table_smem, slot_table, slots,
    kb1, kb2, kb3, kb4, kb5, kb6, kb7,
    vb1, vb2, vb3, vb4, vb5, vb6, vb7,
    stage, got_k, got_v0, got_v1, gathered, scores, weights, totals, out_stage, out_parts,
    load_sem, list_send, list_recv, plan_sem, slot_sem, y_send, y_recv, x_send, x_recv,
    z_send, z_recv, z_local, prev_send, prev_recv, o_send, o_recv, o_local,
):
    seq = lax.axis_index("seq")
    z = lax.axis_index("head")
    y = seq // ROW
    col = seq % ROW
    ahead = (seq + ROW) % (RING * ROW)
    behind = (seq + (RING - 1) * ROW) % (RING * ROW)
    after = (seq + 1) % (RING * ROW)
    before = (seq + RING * ROW - 1) % (RING * ROW)
    blocks_of = ((key_tiles, kb1, kb2, kb3, kb4, kb5, kb6, kb7), (value_tiles, vb1, vb2, vb3, vb4, vb5, vb6, vb7))
    got_v = (got_v0, got_v1)

    def row_peer(o):
        return y * ROW + (col + o) % ROW

    def head_peer(o):
        return (z + o) % HEADS

    pairs = ((keys_hbm, key_tiles), (q_hbm, q_in), (k_hbm, k_in), (v_hbm, v_in), (values_hbm, value_tiles))
    loads = [pltpu.make_async_copy(src, dst, load_sem.at[i]) for i, (src, dst) in enumerate(pairs)]
    for load in loads:
        load.start()

    barrier = pltpu.get_barrier_semaphore()

    def greet(where):
        pl.semaphore_signal(barrier, inc=1, device_id=where, device_id_type=MESH)

    for o in range(1, ROW):
        greet((row_peer(o), z))
    for o in range(1, HEADS):
        greet((seq, head_peer(o)))
    greet((ahead, z))
    greet((behind, z))
    greet((before, HEADS - 2))
    greet((before, HEADS - 1))
    lane = lax.broadcasted_iota(jnp.int32, (ROW, 128), 1)
    device = lax.broadcasted_iota(jnp.int32, (ROW, 128), 0)
    list_raw[...] = jnp.full((8, 128), -1, jnp.int32)
    for block in range(BLOCKS):
        list_raw[pl.ds(block, 1), pl.ds(0, SEL)] = lists[block]
    raw = list_raw[...]
    flat = jnp.full((8, 128), -1, jnp.int32)
    for block in range(BLOCKS):
        moved = pltpu.roll(jnp.broadcast_to(raw[block : block + 1], (8, 128)), block * SEL, 1)
        flat = jnp.where((lane >= block * SEL) & (lane < (block + 1) * SEL), moved, flat)
    list_in[...] = flat

    is_last = z >= HEADS - 2
    pl.semaphore_wait(barrier, ROW - 1 + HEADS - 1 + 2 + jnp.where(is_last, HEADS, 0))

    def remote(src, dst, send, recv, where):
        return pltpu.make_async_remote_copy(
            src_ref=src, dst_ref=dst, send_sem=send, recv_sem=recv, device_id=where, device_id_type=MESH
        )

    def list_copy(o):
        return remote(list_in, row_lists.at[col], list_send.at[o - 1], list_recv.at[o - 1], (row_peer(o), z))

    def ring_copy(kv, way, hop, chunk):
        refs = blocks_of[kv]
        if way == 0:
            src, dst, where = refs[hop - 1], refs[hop], ahead
        else:
            src, dst, where = refs[(RING - hop + 1) % RING], refs[RING - hop], behind
        part = pl.ds(chunk * CHUNK, CHUNK)
        return remote(
            src.at[part], dst.at[part], y_send.at[kv, way, hop - 1, chunk], y_recv.at[kv, way, hop - 1, chunk], (where, z)
        )

    def row_copy(kind, rel, o):
        if kind == 0:
            src, dst = stage.at[0, rel, o - 1], got_k.at[pl.ds((col * RING + rel) * 2, 2)]
        else:
            src, dst = stage.at[1, rel, o - 1, kind - 1], got_v[kind - 1].at[col * RING + rel]
        return remote(src, dst, x_send.at[kind, rel, o - 1], x_recv.at[kind, rel, o - 1], (row_peer(o), z))

    def head_copies(o):
        to = head_peer(o)
        wide = pl.ds(pl.multiple_of(to * WIDE, WIDE), WIDE)
        narrow = pl.ds(pl.multiple_of(to * HD, HD), HD)
        rows = pl.ds(pl.multiple_of(z * PART, PART), PART)
        new_rows = pl.ds(pl.multiple_of(QB + z * PART, PART), PART)
        triples = ((q_in.at[:, wide], q_rows.at[rows]), (k_in.at[:, narrow], k_loc.at[new_rows]), (v_in.at[:, narrow], v_loc.at[new_rows]))
        if o == 0:
            return [pltpu.make_async_copy(src, dst, z_local.at[i]) for i, (src, dst) in enumerate(triples)]
        return [
            remote(src, dst, z_send.at[i, o - 1], z_recv.at[i, o - 1], (seq, to)) for i, (src, dst) in enumerate(triples)
        ]

    def prior_copies(to):
        source = z % 2
        narrow = pl.ds(to * HD, HD)
        rows = pl.ds(pl.multiple_of(source * PART, PART), PART)
        return [
            remote(k_in.at[:, narrow], k_loc.at[rows], prev_send.at[0, to], prev_recv.at[0, source], (after, to)),
            remote(v_in.at[:, narrow], v_loc.at[rows], prev_send.at[1, to], prev_recv.at[1, source], (after, to)),
        ]

    def forward(kv, hop, chunks):
        for chunk in chunks:
            ring_copy(kv, 0, hop, chunk).start()
            ring_copy(kv, 1, hop, chunk).start()

    for o in range(1, ROW):
        list_copy(o).start()
    loads[0].wait()
    forward(0, 1, range(CHUNKS))

    for o in range(1, ROW):
        list_copy(o).wait()
    row_lists[col] = list_in[...]
    listed = row_lists[0]
    for d in range(1, ROW):
        listed = jnp.where(device == d, row_lists[d], listed)
    plan = jnp.zeros((ROW, 128), jnp.int32)
    for rel in range(RING):
        owner = ((y + RING - rel) % RING) * ROW + col
        mine = lax.shift_right_arithmetic(listed, 4) == owner
        tile = jnp.bitwise_and(listed, HELD - 1)
        smallest = jnp.min(jnp.where(mine, tile, HELD - 1), axis=1, keepdims=True)
        largest = jnp.max(jnp.where(mine, tile, 0), axis=1, keepdims=True)
        plan = jnp.where(lane == 2 * rel, smallest, plan)
        plan = jnp.where(lane == 2 * rel + 1, largest, plan)
    table[...] = plan

    def place_own_list():
        entries = BLOCKS * SEL
        across = jnp.broadcast_to(flat[0:1], (entries, 128))
        lanes = lax.broadcasted_iota(jnp.int32, (entries, 128), 1)
        diagonal = lanes == lax.broadcasted_iota(jnp.int32, (entries, 128), 0)
        down = jnp.max(jnp.where(diagonal, across, 0), axis=1, keepdims=True)
        owner = lax.shift_right_arithmetic(down, 4)
        earlier = (lax.shift_right_arithmetic(across, 4) == owner) & (across < down)
        rank = jnp.max(jnp.where(earlier, 1, 0), axis=1, keepdims=True)
        rel = jnp.bitwise_and(y - lax.shift_right_arithmetic(owner, 3), RING - 1)
        slot = (jnp.bitwise_and(owner, ROW - 1) * RING + rel) * 2 + rank
        slot_table[...] = jnp.broadcast_to(slot, (entries, 128))

    left = lax.broadcasted_iota(jnp.int32, (TILE, HD), 1) < HALF

    def halves(lower, upper):
        turned = pltpu.roll(upper, HALF, 1)
        return jnp.where(left, lower, turned), jnp.where(left, turned, lower)

    def pack(kv, rel):
        source = blocks_of[kv][rel]

        def two(to):
            lower = source[jnp.bitwise_and(table_smem[to, 2 * rel], HELD - 1)]
            upper = source[jnp.bitwise_and(table_smem[to, 2 * rel + 1], HELD - 1)]
            return halves(lower, upper) if kv else (lower, upper)

        def one(o, carry):
            first, second = two((col + o) % ROW)
            stage[kv, rel, o - 1, 0] = first
            stage[kv, rel, o - 1, 1] = second
            return carry

        lax.fori_loop(1, ROW, one, 0)
        first, second = two(col)
        place = col * RING + rel
        if kv:
            got_v0[place] = first
            got_v1[place] = second
        else:
            got_k[2 * place] = first
            got_k[2 * place + 1] = second

    def hand_out(kind, rel):
        for o in range(1, ROW):
            row_copy(kind, rel, o).start()

    def hand_in(kind):
        for rel in range(RING):
            for o in range(1, ROW):
                row_copy(kind, rel, o).wait()

    def pass_on(kv, hop, chunk):
        for way in range(2):
            ring_copy(kv, way, hop, chunk).wait_recv()
            if hop < 3 or (chunk < CHUNKS // 2) == (way == 0):
                ring_copy(kv, way, hop + 1, chunk).start()

    def last_block(kv):
        for chunk in range(CHUNKS // 2):
            ring_copy(kv, 0, 4, chunk).wait_recv()
            ring_copy(kv, 1, 4, CHUNKS // 2 + chunk).wait_recv()
        pack(kv, 4)

    def block_at(step):
        return (z // 2 + step) % BLOCKS

    def gather(block, take):
        def one(j, carry):
            slot = jnp.bitwise_and(slots[block * SEL + j, 0], 2 * RING * ROW - 1)
            gathered[pl.ds(pl.multiple_of(j * TILE, TILE), TILE), :] = take(slot)
            return carry

        lax.fori_loop(0, SEL, one, 0)

    row = lax.broadcasted_iota(jnp.int32, (SOFT_ROWS, 2 * QB), 0)
    column = lax.broadcasted_iota(jnp.int32, (SOFT_ROWS, 2 * QB), 1)

    def score(piece, carry):
        step, head = piece // GROUP, piece % GROUP
        block = block_at(step)
        first_row = pl.multiple_of(block * QB, QB)

        @pl.when(head == 0)
        def _():
            gather(block, lambda slot: got_k[slot])
            gathered[pl.ds(REMOTE, 2 * QB), :] = k_loc[pl.ds(first_row, 2 * QB), :]

        query = q_rows[pl.ds(first_row, QB), pl.ds(pl.multiple_of(head * HD, HD), HD)]
        for pair in range(KEYS // (2 * TILE)):
            part = pl.ds(pair * 2 * TILE, 2 * TILE)
            scores[:, part] = lax.dot_general(
                query, gathered[part, :], (((1,), (1,)), ((), ())), preferred_element_type=jnp.float32
            )
        from_column = jnp.where(block + seq > 0, 0, QB)

        def soften(i, inner):
            first = pl.multiple_of(i * SOFT_ROWS, SOFT_ROWS)
            rows = pl.ds(first, SOFT_ROWS)
            kept = pl.ds(pl.multiple_of(head * QB + first, SOFT_ROWS), SOFT_ROWS)
            visible = (column - QB <= row + first) & (column >= from_column)
            far = scores[rows, pl.ds(0, REMOTE)]
            near = jnp.where(visible, scores[rows, pl.ds(REMOTE, 2 * QB)], NEG_FILL)
            top = jnp.maximum(jnp.max(far, axis=1, keepdims=True), jnp.max(near, axis=1, keepdims=True))
            far = jnp.exp2((far - top) * EXP2_SCALE)
            near = jnp.exp2((near - top) * EXP2_SCALE)
            total = jnp.sum(far, axis=1, keepdims=True) + jnp.sum(near, axis=1, keepdims=True)
            weights[step, kept, pl.ds(0, REMOTE)] = far.astype(jnp.bfloat16)
            weights[step, kept, pl.ds(REMOTE, 2 * QB)] = near.astype(jnp.bfloat16)
            totals[step, kept, :] = jnp.broadcast_to(total, (SOFT_ROWS, HD))
            return inner

        return lax.fori_loop(0, QB // SOFT_ROWS, soften, carry)

    place_own_list()
    copy = pltpu.make_async_copy(table, table_smem, plan_sem)
    copy.start()
    for load in loads[1:]:
        load.wait()
    copy.wait()
    pack(0, 0)
    pack(1, 0)
    hand_out(0, 0)
    pass_on(0, 1, 0)
    hand_out(1, 0)
    hand_out(2, 0)
    pass_on(0, 1, 1)
    for o in range(HEADS):
        for copy in head_copies(o):
            copy.start()

    @pl.when(is_last)
    def _():
        for to in range(HEADS):
            for copy in prior_copies(to):
                copy.start()

    pass_on(0, 1, 2)
    pass_on(0, 1, 3)
    for hop in range(1, 4):
        if hop > 1:
            for chunk in range(CHUNKS):
                pass_on(0, hop, chunk)
                if chunk == 0:
                    hand_out(0, RING - hop + 1)
        pack(0, hop)
        pack(0, RING - hop)
        hand_out(0, hop)
    forward(1, 1, range(CHUNKS))
    copy = pltpu.make_async_copy(slot_table, slots, slot_sem)
    copy.start()
    copy.wait()
    hand_out(0, 5)
    last_block(0)

    pass_on(1, 1, 0)
    hand_out(0, 4)
    for chunk in range(1, CHUNKS):
        pass_on(1, 1, chunk)
    for o in range(HEADS):
        for copy in head_copies(o):
            copy.wait()
    for source in range(2):
        rows = pl.ds(source * PART, PART)
        for kv, ref in enumerate((k_loc, v_loc)):
            pltpu.make_async_copy(ref.at[rows], ref.at[rows], prev_recv.at[kv, source]).wait()
    pack(1, 1)
    pack(1, 7)
    hand_out(1, 1)
    hand_out(2, 1)
    done = 0
    for hop in range(2, 4):
        for chunk in range(CHUNKS):
            pass_on(1, hop, chunk)
            if hop == 2 and chunk == 0:
                hand_out(1, 7)
                hand_out(2, 7)
                continue
            if hop == 2 and chunk == 1:
                hand_in(0)
            if hop == 3 and chunk == 0:
                hand_out(1, 6)
                hand_out(2, 6)
            lax.fori_loop(done, done + 2, score, 0)
            done += 2
        pack(1, hop)
        pack(1, RING - hop)
        hand_out(1, hop)
        if hop == 2:
            hand_out(2, hop)
    hand_out(1, 5)
    lax.fori_loop(done, BLOCKS * GROUP, score, 0)
    last_block(1)
    hand_out(2, 3)
    hand_out(1, 4)
    hand_out(2, 5)
    hand_out(2, 4)

    def attend(step, half):
        block = block_at(step)
        first_row = pl.multiple_of(block * QB, QB)

        def take(slot):
            on_left = jnp.bitwise_and(slot, 1) == half
            return jnp.where(left == on_left, got_v[half][lax.shift_right_logical(slot, 1)], zero)

        zero = jnp.zeros((TILE, HD), jnp.bfloat16)
        gather(block, take)
        near = v_loc[pl.ds(first_row, 2 * QB), :]
        near_left = lax.broadcasted_iota(jnp.int32, (2 * QB, HD), 1) < HALF
        gathered[pl.ds(REMOTE, 2 * QB), :] = jnp.where(near_left == (half == 0), near, jnp.zeros_like(near))
        sides = jnp.dot(weights[step], gathered[...], preferred_element_type=jnp.float32)
        result = ((sides + pltpu.roll(sides, HALF, 1)) / totals[step]).astype(jnp.bfloat16)
        for pair in range(GROUP // 2):
            even, odd = result[2 * pair * QB : (2 * pair + 1) * QB], result[(2 * pair + 1) * QB : (2 * pair + 2) * QB]
            out_stage[half, pl.ds(first_row, QB), pl.ds(pair * HD, HD)] = jnp.where(left, even, odd)

    def return_copy(step, half, to, place):
        rows = pl.ds(pl.multiple_of(to * PART, PART), PART)
        part = pl.ds(pl.multiple_of(z * (WIDE // 2), WIDE // 2), WIDE // 2)
        src, dst = out_stage.at[half, rows], out_parts.at[half, :, part]
        if place is None:
            return pltpu.make_async_copy(src, dst, o_local.at[half])
        return remote(src, dst, o_send.at[half, place], o_recv.at[half, place], (seq, to))

    returns = []
    for half in range(2):
        hand_in(1 + half)
        for step in ORDER:
            attend(step, half)
            if step != 0:
                for parity in range(2):
                    to = 2 * block_at(step) + parity
                    returns.append(return_copy(step, half, to, 2 * step + (z + parity) % 2))
            else:
                returns.append(return_copy(step, half, z + 1 - 2 * (z % 2), 0))
                returns.append(return_copy(step, half, z, None))
            returns[-2].start()
            returns[-1].start()
    for copy in returns:
        copy.wait()

    part_left = lax.broadcasted_iota(jnp.int32, (PART, HD), 1) < HALF
    for pair in range(HEADS * GROUP // 2):
        lanes = pl.ds(pair * HD, HD)
        first, second = out_parts[0, :, lanes], out_parts[1, :, lanes]
        out[:, pl.ds(2 * pair * HD, HD)] = jnp.where(part_left, first, pltpu.roll(second, HALF, 1))
        out[:, pl.ds((2 * pair + 1) * HD, HD)] = jnp.where(part_left, pltpu.roll(first, HALF, 1), second)

    for kv in range(2):
        for hop in range(1, 5):
            for chunk in range(CHUNKS):
                for way in range(2):
                    if hop < 4 or (chunk < CHUNKS // 2) == (way == 0):
                        ring_copy(kv, way, hop, chunk).wait_send()

    @pl.when(is_last)
    def _():
        for to in range(HEADS):
            for copy in prior_copies(to):
                copy.wait_send()


def on_device(queries, new_keys, new_values, cache_keys, cache_values, tile_lists):
    tiles = pltpu.VMEM((HELD, TILE, HD), jnp.bfloat16)
    dma = pltpu.SemaphoreType.DMA
    vmem = pl.BlockSpec(memory_space=pltpu.VMEM)
    return pl.pallas_call(
        kernel,
        out_shape=pltpu.VMEM((PART, HEADS * WIDE), jnp.bfloat16),
        in_specs=[pl.BlockSpec(memory_space=pl.ANY)] * 5 + [vmem],
        out_specs=vmem,
        scratch_shapes=[
            pltpu.VMEM((PART, HEADS * WIDE), jnp.bfloat16),
            pltpu.VMEM((PART, HEADS * HD), jnp.bfloat16),
            pltpu.VMEM((PART, HEADS * HD), jnp.bfloat16),
            tiles,
            tiles,
            pltpu.VMEM((ROWS, WIDE), jnp.bfloat16),
            pltpu.VMEM((QB + ROWS, HD), jnp.bfloat16),
            pltpu.VMEM((QB + ROWS, HD), jnp.bfloat16),
            pltpu.VMEM((8, 128), jnp.int32),
            pltpu.VMEM((8, 128), jnp.int32),
            pltpu.VMEM((ROW, 8, 128), jnp.int32),
            pltpu.VMEM((ROW, 128), jnp.int32),
            pltpu.SMEM((ROW, 128), jnp.int32),
            pltpu.VMEM((BLOCKS * SEL, 128), jnp.int32),
            pltpu.SMEM((BLOCKS * SEL, 128), jnp.int32),
            *([tiles] * 14),
            pltpu.VMEM((2, RING, ROW - 1, 2, TILE, HD), jnp.bfloat16),
            pltpu.VMEM((2 * RING * ROW, TILE, HD), jnp.bfloat16),
            pltpu.VMEM((RING * ROW, TILE, HD), jnp.bfloat16),
            pltpu.VMEM((RING * ROW, TILE, HD), jnp.bfloat16),
            pltpu.VMEM((KEYS, HD), jnp.bfloat16),
            pltpu.VMEM((QB, KEYS), jnp.float32),
            pltpu.VMEM((BLOCKS, GROUP * QB, KEYS), jnp.bfloat16),
            pltpu.VMEM((BLOCKS, GROUP * QB, HD), jnp.float32),
            pltpu.VMEM((2, ROWS, WIDE // 2), jnp.bfloat16),
            pltpu.VMEM((2, PART, HEADS * WIDE // 2), jnp.bfloat16),
            dma((5,)),
            dma((ROW - 1,)),
            dma((ROW - 1,)),
            dma,
            dma,
            dma((2, 2, 4, CHUNKS)),
            dma((2, 2, 4, CHUNKS)),
            dma((3, RING, ROW - 1)),
            dma((3, RING, ROW - 1)),
            dma((3, HEADS - 1)),
            dma((3, HEADS - 1)),
            dma((3,)),
            dma((2, HEADS)),
            dma((2, 2)),
            dma((2, HEADS)),
            dma((2, HEADS)),
            dma((2,)),
        ],
        compiler_params=pltpu.CompilerParams(
            collective_id=0, has_side_effects=True, vmem_limit_bytes=64000 * 1024
        ),
    )(
        queries,
        new_keys,
        new_values,
        cache_keys.reshape(HELD, TILE, HD),
        cache_values.reshape(HELD, TILE, HD),
        tile_lists,
    )


def solution(mesh):
    return jax.shard_map(
        on_device,
        mesh=mesh,
        in_specs=(
            P(("seq", "head"), None),
            P(("seq", "head"), None),
            P(("seq", "head"), None),
            P("seq", "head"),
            P("seq", "head"),
            P("seq", "head", None),
        ),
        out_specs=P(("seq", "head"), None),
        check_vma=False,
    )
```

```python
import functools
import math

import jax
import jax.numpy as jnp
from jax import lax
from jax.experimental import pallas as pl
from jax.experimental.pallas import tpu as pltpu
from jax.sharding import PartitionSpec as P

KV = 8
HD = 128
QB = 128
TILE = 128
SEL = 12
GROUP = 4

RING = 8
ROW = 8
HEADS = 8
HELD = 16
CHUNK = 4
CHUNKS = HELD // CHUNK
BLOCKS = 4
ROWS = BLOCKS * QB
PART = ROWS // HEADS
WIDE = GROUP * HD
HALF = HD // 2
REMOTE = SEL * TILE
KEYS = REMOTE + 2 * QB
NEG_FILL = -1e30
EXP2_SCALE = math.log2(math.e) / math.sqrt(HD)
MESH = pl.DeviceIdType.MESH
ORDER = (2, 1, 3, 0)
SOFT_ROWS = 32


def kernel(
    q_hbm, k_hbm, v_hbm, keys_hbm, values_hbm, lists,
    out,
    q_in, k_in, v_in, key_tiles, value_tiles, q_rows, k_loc, v_loc, list_raw, list_in, row_lists, table, table_smem, slot_table, slots,
    kb1, kb2, kb3, kb4, kb5, kb6, kb7,
    vb1, vb2, vb3, vb4, vb5, vb6, vb7,
    stage, got_k, got_v0, got_v1, gathered, scores, weights, totals, out_stage, out_parts,
    load_sem, list_send, list_recv, plan_sem, slot_sem, y_send, y_recv, x_send, x_recv,
    z_send, z_recv, z_local, prev_send, prev_recv, o_send, o_recv, o_local,
):
    seq = lax.axis_index("seq")
    z = lax.axis_index("head")
    y = seq // ROW
    col = seq % ROW
    ahead = (seq + ROW) % (RING * ROW)
    behind = (seq + (RING - 1) * ROW) % (RING * ROW)
    after = (seq + 1) % (RING * ROW)
    before = (seq + RING * ROW - 1) % (RING * ROW)
    blocks_of = ((key_tiles, kb1, kb2, kb3, kb4, kb5, kb6, kb7), (value_tiles, vb1, vb2, vb3, vb4, vb5, vb6, vb7))
    got_v = (got_v0, got_v1)

    def row_peer(o):
        return y * ROW + (col + o) % ROW

    def head_peer(o):
        return (z + o) % HEADS

    pairs = ((keys_hbm, key_tiles), (q_hbm, q_in), (k_hbm, k_in), (v_hbm, v_in), (values_hbm, value_tiles))
    loads = [pltpu.make_async_copy(src, dst, load_sem.at[i]) for i, (src, dst) in enumerate(pairs)]
    for load in loads:
        load.start()

    barrier = pltpu.get_barrier_semaphore()

    def greet(where):
        pl.semaphore_signal(barrier, inc=1, device_id=where, device_id_type=MESH)

    for o in range(1, ROW):
        greet((row_peer(o), z))
    for o in range(1, HEADS):
        greet((seq, head_peer(o)))
    greet((ahead, z))
    greet((behind, z))
    greet((before, HEADS - 2))
    greet((before, HEADS - 1))
    lane = lax.broadcasted_iota(jnp.int32, (ROW, 128), 1)
    device = lax.broadcasted_iota(jnp.int32, (ROW, 128), 0)
    list_raw[...] = jnp.full((8, 128), -1, jnp.int32)
    for block in range(BLOCKS):
        list_raw[pl.ds(block, 1), pl.ds(0, SEL)] = lists[block]
    raw = list_raw[...]
    flat = jnp.full((8, 128), -1, jnp.int32)
    for block in range(BLOCKS):
        moved = pltpu.roll(jnp.broadcast_to(raw[block : block + 1], (8, 128)), block * SEL, 1)
        flat = jnp.where((lane >= block * SEL) & (lane < (block + 1) * SEL), moved, flat)
    list_in[...] = flat

    is_last = z >= HEADS - 2
    pl.semaphore_wait(barrier, ROW - 1 + HEADS - 1 + 2 + jnp.where(is_last, HEADS, 0))

    def remote(src, dst, send, recv, where):
        return pltpu.make_async_remote_copy(
            src_ref=src, dst_ref=dst, send_sem=send, recv_sem=recv, device_id=where, device_id_type=MESH
        )

    def list_copy(o):
        return remote(list_in, row_lists.at[col], list_send.at[o - 1], list_recv.at[o - 1], (row_peer(o), z))

    def ring_copy(kv, way, hop, chunk):
        refs = blocks_of[kv]
        if way == 0:
            src, dst, where = refs[hop - 1], refs[hop], ahead
        else:
            src, dst, where = refs[(RING - hop + 1) % RING], refs[RING - hop], behind
        part = pl.ds(chunk * CHUNK, CHUNK)
        return remote(
            src.at[part], dst.at[part], y_send.at[kv, way, hop - 1, chunk], y_recv.at[kv, way, hop - 1, chunk], (where, z)
        )

    def row_copy(kind, rel, o):
        if kind == 0:
            src, dst = stage.at[0, rel, o - 1], got_k.at[pl.ds((col * RING + rel) * 2, 2)]
        else:
            src, dst = stage.at[1, rel, o - 1, kind - 1], got_v[kind - 1].at[col * RING + rel]
        return remote(src, dst, x_send.at[kind, rel, o - 1], x_recv.at[kind, rel, o - 1], (row_peer(o), z))

    def head_copies(o):
        to = head_peer(o)
        wide = pl.ds(pl.multiple_of(to * WIDE, WIDE), WIDE)
        narrow = pl.ds(pl.multiple_of(to * HD, HD), HD)
        rows = pl.ds(pl.multiple_of(z * PART, PART), PART)
        new_rows = pl.ds(pl.multiple_of(QB + z * PART, PART), PART)
        triples = ((q_in.at[:, wide], q_rows.at[rows]), (k_in.at[:, narrow], k_loc.at[new_rows]), (v_in.at[:, narrow], v_loc.at[new_rows]))
        if o == 0:
            return [pltpu.make_async_copy(src, dst, z_local.at[i]) for i, (src, dst) in enumerate(triples)]
        return [
            remote(src, dst, z_send.at[i, o - 1], z_recv.at[i, o - 1], (seq, to)) for i, (src, dst) in enumerate(triples)
        ]

    def prior_copies(to):
        source = z % 2
        narrow = pl.ds(to * HD, HD)
        rows = pl.ds(pl.multiple_of(source * PART, PART), PART)
        return [
            remote(k_in.at[:, narrow], k_loc.at[rows], prev_send.at[0, to], prev_recv.at[0, source], (after, to)),
            remote(v_in.at[:, narrow], v_loc.at[rows], prev_send.at[1, to], prev_recv.at[1, source], (after, to)),
        ]

    def forward(kv, hop, chunks):
        for chunk in chunks:
            ring_copy(kv, 0, hop, chunk).start()
            ring_copy(kv, 1, hop, chunk).start()

    for o in range(1, ROW):
        list_copy(o).start()
    loads[0].wait()
    forward(0, 1, range(CHUNKS))

    for o in range(1, ROW):
        list_copy(o).wait()
    row_lists[col] = list_in[...]
    listed = row_lists[0]
    for d in range(1, ROW):
        listed = jnp.where(device == d, row_lists[d], listed)
    plan = jnp.zeros((ROW, 128), jnp.int32)
    for rel in range(RING):
        owner = ((y + RING - rel) % RING) * ROW + col
        mine = lax.shift_right_arithmetic(listed, 4) == owner
        tile = jnp.bitwise_and(listed, HELD - 1)
        smallest = jnp.min(jnp.where(mine, tile, HELD - 1), axis=1, keepdims=True)
        largest = jnp.max(jnp.where(mine, tile, 0), axis=1, keepdims=True)
        plan = jnp.where(lane == 2 * rel, smallest, plan)
        plan = jnp.where(lane == 2 * rel + 1, largest, plan)
    table[...] = plan

    def place_own_list():
        entries = BLOCKS * SEL
        across = jnp.broadcast_to(flat[0:1], (entries, 128))
        lanes = lax.broadcasted_iota(jnp.int32, (entries, 128), 1)
        diagonal = lanes == lax.broadcasted_iota(jnp.int32, (entries, 128), 0)
        down = jnp.max(jnp.where(diagonal, across, 0), axis=1, keepdims=True)
        owner = lax.shift_right_arithmetic(down, 4)
        earlier = (lax.shift_right_arithmetic(across, 4) == owner) & (across < down)
        rank = jnp.max(jnp.where(earlier, 1, 0), axis=1, keepdims=True)
        rel = jnp.bitwise_and(y - lax.shift_right_arithmetic(owner, 3), RING - 1)
        slot = (jnp.bitwise_and(owner, ROW - 1) * RING + rel) * 2 + rank
        slot_table[...] = jnp.broadcast_to(slot, (entries, 128))

    left = lax.broadcasted_iota(jnp.int32, (TILE, HD), 1) < HALF

    def halves(lower, upper):
        turned = pltpu.roll(upper, HALF, 1)
        return jnp.where(left, lower, turned), jnp.where(left, turned, lower)

    def pack(kv, rel):
        source = blocks_of[kv][rel]

        def two(to):
            lower = source[jnp.bitwise_and(table_smem[to, 2 * rel], HELD - 1)]
            upper = source[jnp.bitwise_and(table_smem[to, 2 * rel + 1], HELD - 1)]
            return halves(lower, upper) if kv else (lower, upper)

        def one(o, carry):
            first, second = two((col + o) % ROW)
            stage[kv, rel, o - 1, 0] = first
            stage[kv, rel, o - 1, 1] = second
            return carry

        lax.fori_loop(1, ROW, one, 0, unroll=True)
        first, second = two(col)
        place = col * RING + rel
        if kv:
            got_v0[place] = first
            got_v1[place] = second
        else:
            got_k[2 * place] = first
            got_k[2 * place + 1] = second

    def hand_out(kind, rel):
        for o in range(1, ROW):
            row_copy(kind, rel, o).start()

    def hand_in(kind):
        for rel in range(RING):
            for o in range(1, ROW):
                row_copy(kind, rel, o).wait()

    def pass_on(kv, hop, chunk):
        for way in range(2):
            ring_copy(kv, way, hop, chunk).wait_recv()
            if hop < 3 or (chunk < CHUNKS // 2) == (way == 0):
                ring_copy(kv, way, hop + 1, chunk).start()

    def last_block(kv):
        for chunk in range(CHUNKS // 2):
            ring_copy(kv, 0, 4, chunk).wait_recv()
            ring_copy(kv, 1, 4, CHUNKS // 2 + chunk).wait_recv()
        pack(kv, 4)

    def block_at(step):
        return (z // 2 + step) % BLOCKS

    def gather(block, take):
        def one(j, carry):
            slot = jnp.bitwise_and(slots[block * SEL + j, 0], 2 * RING * ROW - 1)
            gathered[pl.ds(pl.multiple_of(j * TILE, TILE), TILE), :] = take(slot)
            return carry

        lax.fori_loop(0, SEL, one, 0, unroll=True)

    row = lax.broadcasted_iota(jnp.int32, (SOFT_ROWS, 2 * QB), 0)
    column = lax.broadcasted_iota(jnp.int32, (SOFT_ROWS, 2 * QB), 1)

    def score(piece, carry):
        step, head = piece // GROUP, piece % GROUP
        block = block_at(step)
        first_row = pl.multiple_of(block * QB, QB)

        @pl.when(head == 0)
        def _():
            gather(block, lambda slot: got_k[slot])
            gathered[pl.ds(REMOTE, 2 * QB), :] = k_loc[pl.ds(first_row, 2 * QB), :]

        query = q_rows[pl.ds(first_row, QB), pl.ds(pl.multiple_of(head * HD, HD), HD)]
        for pair in range(KEYS // (2 * TILE)):
            part = pl.ds(pair * 2 * TILE, 2 * TILE)
            scores[:, part] = lax.dot_general(
                query, gathered[part, :], (((1,), (1,)), ((), ())), preferred_element_type=jnp.float32
            )
        from_column = jnp.where(block + seq > 0, 0, QB)

        def soften(i, inner):
            first = pl.multiple_of(i * SOFT_ROWS, SOFT_ROWS)
            rows = pl.ds(first, SOFT_ROWS)
            kept = pl.ds(pl.multiple_of(head * QB + first, SOFT_ROWS), SOFT_ROWS)
            visible = (column - QB <= row + first) & (column >= from_column)
            far = scores[rows, pl.ds(0, REMOTE)]
            near = jnp.where(visible, scores[rows, pl.ds(REMOTE, 2 * QB)], NEG_FILL)
            top = jnp.maximum(jnp.max(far, axis=1, keepdims=True), jnp.max(near, axis=1, keepdims=True))
            far = jnp.exp2((far - top) * EXP2_SCALE)
            near = jnp.exp2((near - top) * EXP2_SCALE)
            total = jnp.sum(far, axis=1, keepdims=True) + jnp.sum(near, axis=1, keepdims=True)
            weights[step, kept, pl.ds(0, REMOTE)] = far.astype(jnp.bfloat16)
            weights[step, kept, pl.ds(REMOTE, 2 * QB)] = near.astype(jnp.bfloat16)
            totals[step, kept, :] = jnp.broadcast_to(total, (SOFT_ROWS, HD))
            return inner

        return lax.fori_loop(0, QB // SOFT_ROWS, soften, carry)

    place_own_list()
    copy = pltpu.make_async_copy(table, table_smem, plan_sem)
    copy.start()
    for load in loads[1:]:
        load.wait()
    copy.wait()
    pack(0, 0)
    pack(1, 0)
    hand_out(0, 0)
    pass_on(0, 1, 0)
    hand_out(1, 0)
    hand_out(2, 0)
    pass_on(0, 1, 1)
    for o in range(HEADS):
        for copy in head_copies(o):
            copy.start()

    @pl.when(is_last)
    def _():
        for to in range(HEADS):
            for copy in prior_copies(to):
                copy.start()

    pass_on(0, 1, 2)
    pass_on(0, 1, 3)
    for hop in range(1, 4):
        if hop > 1:
            for chunk in range(CHUNKS):
                pass_on(0, hop, chunk)
                if chunk == 0:
                    hand_out(0, RING - hop + 1)
        pack(0, hop)
        pack(0, RING - hop)
        hand_out(0, hop)
    forward(1, 1, range(CHUNKS))
    copy = pltpu.make_async_copy(slot_table, slots, slot_sem)
    copy.start()
    copy.wait()
    hand_out(0, 5)
    last_block(0)

    pass_on(1, 1, 0)
    hand_out(0, 4)
    for chunk in range(1, CHUNKS):
        pass_on(1, 1, chunk)
    for o in range(HEADS):
        for copy in head_copies(o):
            copy.wait()
    for source in range(2):
        rows = pl.ds(source * PART, PART)
        for kv, ref in enumerate((k_loc, v_loc)):
            pltpu.make_async_copy(ref.at[rows], ref.at[rows], prev_recv.at[kv, source]).wait()
    pack(1, 1)
    pack(1, 7)
    hand_out(1, 1)
    hand_out(2, 1)
    done = 0
    for hop in range(2, 4):
        for chunk in range(CHUNKS):
            pass_on(1, hop, chunk)
            if hop == 2 and chunk == 0:
                hand_out(1, 7)
                hand_out(2, 7)
                continue
            if hop == 2 and chunk == 1:
                hand_in(0)
            if hop == 3 and chunk == 0:
                hand_out(1, 6)
                hand_out(2, 6)
            lax.fori_loop(done, done + 2, score, 0)
            done += 2
        pack(1, hop)
        pack(1, RING - hop)
        hand_out(1, hop)
        if hop == 2:
            hand_out(2, hop)
    hand_out(1, 5)
    lax.fori_loop(done, BLOCKS * GROUP, score, 0)
    last_block(1)
    hand_out(2, 3)
    hand_out(1, 4)
    hand_out(2, 5)
    hand_out(2, 4)

    def attend(step, half):
        block = block_at(step)
        first_row = pl.multiple_of(block * QB, QB)

        def take(slot):
            on_left = jnp.bitwise_and(slot, 1) == half
            return jnp.where(left == on_left, got_v[half][lax.shift_right_logical(slot, 1)], zero)

        zero = jnp.zeros((TILE, HD), jnp.bfloat16)
        gather(block, take)
        near = v_loc[pl.ds(first_row, 2 * QB), :]
        near_left = lax.broadcasted_iota(jnp.int32, (2 * QB, HD), 1) < HALF
        gathered[pl.ds(REMOTE, 2 * QB), :] = jnp.where(near_left == (half == 0), near, jnp.zeros_like(near))
        sides = jnp.dot(weights[step], gathered[...], preferred_element_type=jnp.float32)
        result = ((sides + pltpu.roll(sides, HALF, 1)) / totals[step]).astype(jnp.bfloat16)
        for pair in range(GROUP // 2):
            even, odd = result[2 * pair * QB : (2 * pair + 1) * QB], result[(2 * pair + 1) * QB : (2 * pair + 2) * QB]
            out_stage[half, pl.ds(first_row, QB), pl.ds(pair * HD, HD)] = jnp.where(left, even, odd)

    def return_copy(step, half, to, place):
        rows = pl.ds(pl.multiple_of(to * PART, PART), PART)
        part = pl.ds(pl.multiple_of(z * (WIDE // 2), WIDE // 2), WIDE // 2)
        src, dst = out_stage.at[half, rows], out_parts.at[half, :, part]
        if place is None:
            return pltpu.make_async_copy(src, dst, o_local.at[half])
        return remote(src, dst, o_send.at[half, place], o_recv.at[half, place], (seq, to))

    returns = []
    for half in range(2):
        hand_in(1 + half)
        for step in ORDER:
            attend(step, half)
            if step != 0:
                for parity in range(2):
                    to = 2 * block_at(step) + parity
                    returns.append(return_copy(step, half, to, 2 * step + (z + parity) % 2))
            else:
                returns.append(return_copy(step, half, z + 1 - 2 * (z % 2), 0))
                returns.append(return_copy(step, half, z, None))
            returns[-2].start()
            returns[-1].start()
    for copy in returns:
        copy.wait()

    part_left = lax.broadcasted_iota(jnp.int32, (PART, HD), 1) < HALF
    for pair in range(HEADS * GROUP // 2):
        lanes = pl.ds(pair * HD, HD)
        first, second = out_parts[0, :, lanes], out_parts[1, :, lanes]
        out[:, pl.ds(2 * pair * HD, HD)] = jnp.where(part_left, first, pltpu.roll(second, HALF, 1))
        out[:, pl.ds((2 * pair + 1) * HD, HD)] = jnp.where(part_left, pltpu.roll(first, HALF, 1), second)

    for kv in range(2):
        for hop in range(1, 5):
            for chunk in range(CHUNKS):
                for way in range(2):
                    if hop < 4 or (chunk < CHUNKS // 2) == (way == 0):
                        ring_copy(kv, way, hop, chunk).wait_send()

    @pl.when(is_last)
    def _():
        for to in range(HEADS):
            for copy in prior_copies(to):
                copy.wait_send()


def on_device(queries, new_keys, new_values, cache_keys, cache_values, tile_lists):
    tiles = pltpu.VMEM((HELD, TILE, HD), jnp.bfloat16)
    dma = pltpu.SemaphoreType.DMA
    vmem = pl.BlockSpec(memory_space=pltpu.VMEM)
    return pl.pallas_call(
        kernel,
        out_shape=pltpu.VMEM((PART, HEADS * WIDE), jnp.bfloat16),
        in_specs=[pl.BlockSpec(memory_space=pl.ANY)] * 5 + [vmem],
        out_specs=vmem,
        scratch_shapes=[
            pltpu.VMEM((PART, HEADS * WIDE), jnp.bfloat16),
            pltpu.VMEM((PART, HEADS * HD), jnp.bfloat16),
            pltpu.VMEM((PART, HEADS * HD), jnp.bfloat16),
            tiles,
            tiles,
            pltpu.VMEM((ROWS, WIDE), jnp.bfloat16),
            pltpu.VMEM((QB + ROWS, HD), jnp.bfloat16),
            pltpu.VMEM((QB + ROWS, HD), jnp.bfloat16),
            pltpu.VMEM((8, 128), jnp.int32),
            pltpu.VMEM((8, 128), jnp.int32),
            pltpu.VMEM((ROW, 8, 128), jnp.int32),
            pltpu.VMEM((ROW, 128), jnp.int32),
            pltpu.SMEM((ROW, 128), jnp.int32),
            pltpu.VMEM((BLOCKS * SEL, 128), jnp.int32),
            pltpu.SMEM((BLOCKS * SEL, 128), jnp.int32),
            *([tiles] * 14),
            pltpu.VMEM((2, RING, ROW - 1, 2, TILE, HD), jnp.bfloat16),
            pltpu.VMEM((2 * RING * ROW, TILE, HD), jnp.bfloat16),
            pltpu.VMEM((RING * ROW, TILE, HD), jnp.bfloat16),
            pltpu.VMEM((RING * ROW, TILE, HD), jnp.bfloat16),
            pltpu.VMEM((KEYS, HD), jnp.bfloat16),
            pltpu.VMEM((QB, KEYS), jnp.float32),
            pltpu.VMEM((BLOCKS, GROUP * QB, KEYS), jnp.bfloat16),
            pltpu.VMEM((BLOCKS, GROUP * QB, HD), jnp.float32),
            pltpu.VMEM((2, ROWS, WIDE // 2), jnp.bfloat16),
            pltpu.VMEM((2, PART, HEADS * WIDE // 2), jnp.bfloat16),
            dma((5,)),
            dma((ROW - 1,)),
            dma((ROW - 1,)),
            dma,
            dma,
            dma((2, 2, 4, CHUNKS)),
            dma((2, 2, 4, CHUNKS)),
            dma((3, RING, ROW - 1)),
            dma((3, RING, ROW - 1)),
            dma((3, HEADS - 1)),
            dma((3, HEADS - 1)),
            dma((3,)),
            dma((2, HEADS)),
            dma((2, 2)),
            dma((2, HEADS)),
            dma((2, HEADS)),
            dma((2,)),
        ],
        compiler_params=pltpu.CompilerParams(
            collective_id=0, has_side_effects=True, vmem_limit_bytes=64000 * 1024
        ),
    )(
        queries,
        new_keys,
        new_values,
        cache_keys.reshape(HELD, TILE, HD),
        cache_values.reshape(HELD, TILE, HD),
        tile_lists,
    )


def solution(mesh):
    return jax.shard_map(
        on_device,
        mesh=mesh,
        in_specs=(
            P(("seq", "head"), None),
            P(("seq", "head"), None),
            P(("seq", "head"), None),
            P("seq", "head"),
            P("seq", "head"),
            P("seq", "head", None),
        ),
        out_specs=P(("seq", "head"), None),
        check_vma=False,
    )
```

```python
import functools
import math

import jax
import jax.numpy as jnp
from jax import lax
from jax.experimental import pallas as pl
from jax.experimental.pallas import tpu as pltpu
from jax.sharding import PartitionSpec as P

KV = 8
HD = 128
QB = 128
TILE = 128
SEL = 12
GROUP = 4

RING = 8
ROW = 8
HEADS = 8
HELD = 16
CHUNK = 4
CHUNKS = HELD // CHUNK
BLOCKS = 4
ROWS = BLOCKS * QB
PART = ROWS // HEADS
WIDE = GROUP * HD
HALF = HD // 2
REMOTE = SEL * TILE
KEYS = REMOTE + 2 * QB
NEG_FILL = -1e30
EXP2_SCALE = math.log2(math.e) / math.sqrt(HD)
MESH = pl.DeviceIdType.MESH
ORDER = (1, 3, 2, 0)
SOFT_ROWS = 32


def kernel(
    q_hbm, k_hbm, v_hbm, keys_hbm, values_hbm, lists,
    out,
    q_in, k_in, v_in, key_tiles, value_tiles, q_rows, k_loc, v_loc, list_raw, list_in, row_lists, table, table_smem, slot_table, slots,
    kb1, kb2, kb3, kb4, kb5, kb6, kb7,
    vb1, vb2, vb3, vb4, vb5, vb6, vb7,
    stage, got_k, got_v0, got_v1, gathered, scores, weights, inverses, out_stage, out_parts,
    load_sem, list_send, list_recv, plan_sem, slot_sem, y_send, y_recv, x_send, x_recv,
    z_send, z_recv, z_local, prev_send, prev_recv, o_send, o_recv, o_local,
):
    seq = lax.axis_index("seq")
    z = lax.axis_index("head")
    y = seq // ROW
    col = seq % ROW
    ahead = (seq + ROW) % (RING * ROW)
    behind = (seq + (RING - 1) * ROW) % (RING * ROW)
    after = (seq + 1) % (RING * ROW)
    before = (seq + RING * ROW - 1) % (RING * ROW)
    blocks_of = ((key_tiles, kb1, kb2, kb3, kb4, kb5, kb6, kb7), (value_tiles, vb1, vb2, vb3, vb4, vb5, vb6, vb7))
    got_v = (got_v0, got_v1)

    def row_peer(o):
        return y * ROW + (col + o) % ROW

    def head_peer(o):
        return (z + o) % HEADS

    pairs = ((keys_hbm, key_tiles), (q_hbm, q_in), (k_hbm, k_in), (v_hbm, v_in), (values_hbm, value_tiles))
    loads = [pltpu.make_async_copy(src, dst, load_sem.at[i]) for i, (src, dst) in enumerate(pairs)]
    for load in loads:
        load.start()

    barrier = pltpu.get_barrier_semaphore()

    def greet(where):
        pl.semaphore_signal(barrier, inc=1, device_id=where, device_id_type=MESH)

    for o in range(1, ROW):
        greet((row_peer(o), z))
    for o in range(1, HEADS):
        greet((seq, head_peer(o)))
    greet((ahead, z))
    greet((behind, z))
    greet((before, HEADS - 2))
    greet((before, HEADS - 1))
    lane = lax.broadcasted_iota(jnp.int32, (ROW, 128), 1)
    device = lax.broadcasted_iota(jnp.int32, (ROW, 128), 0)
    list_raw[...] = jnp.full((8, 128), -1, jnp.int32)
    for block in range(BLOCKS):
        list_raw[pl.ds(block, 1), pl.ds(0, SEL)] = lists[block]
    raw = list_raw[...]
    flat = jnp.full((8, 128), -1, jnp.int32)
    for block in range(BLOCKS):
        moved = pltpu.roll(jnp.broadcast_to(raw[block : block + 1], (8, 128)), block * SEL, 1)
        flat = jnp.where((lane >= block * SEL) & (lane < (block + 1) * SEL), moved, flat)
    list_in[...] = flat

    is_last = z >= HEADS - 2
    pl.semaphore_wait(barrier, ROW - 1 + HEADS - 1 + 2 + jnp.where(is_last, HEADS, 0))

    def remote(src, dst, send, recv, where):
        return pltpu.make_async_remote_copy(
            src_ref=src, dst_ref=dst, send_sem=send, recv_sem=recv, device_id=where, device_id_type=MESH
        )

    def list_copy(o):
        return remote(list_in, row_lists.at[col], list_send.at[o - 1], list_recv.at[o - 1], (row_peer(o), z))

    def ring_copy(kv, way, hop, chunk):
        refs = blocks_of[kv]
        if way == 0:
            src, dst, where = refs[hop - 1], refs[hop], ahead
        else:
            src, dst, where = refs[(RING - hop + 1) % RING], refs[RING - hop], behind
        part = pl.ds(chunk * CHUNK, CHUNK)
        return remote(
            src.at[part], dst.at[part], y_send.at[kv, way, hop - 1, chunk], y_recv.at[kv, way, hop - 1, chunk], (where, z)
        )

    def row_copy(kind, rel, o):
        if kind == 0:
            src, dst = stage.at[0, rel, o - 1], got_k.at[pl.ds((col * RING + rel) * 2, 2)]
        else:
            src, dst = stage.at[1, rel, o - 1, kind - 1], got_v[kind - 1].at[col * RING + rel]
        return remote(src, dst, x_send.at[kind, rel, o - 1], x_recv.at[kind, rel, o - 1], (row_peer(o), z))

    def head_copies(o):
        to = head_peer(o)
        wide = pl.ds(pl.multiple_of(to * WIDE, WIDE), WIDE)
        narrow = pl.ds(pl.multiple_of(to * HD, HD), HD)
        rows = pl.ds(pl.multiple_of(z * PART, PART), PART)
        new_rows = pl.ds(pl.multiple_of(QB + z * PART, PART), PART)
        triples = ((q_in.at[:, wide], q_rows.at[rows]), (k_in.at[:, narrow], k_loc.at[new_rows]), (v_in.at[:, narrow], v_loc.at[new_rows]))
        if o == 0:
            return [pltpu.make_async_copy(src, dst, z_local.at[i]) for i, (src, dst) in enumerate(triples)]
        return [
            remote(src, dst, z_send.at[i, o - 1], z_recv.at[i, o - 1], (seq, to)) for i, (src, dst) in enumerate(triples)
        ]

    def prior_copies(to):
        source = z % 2
        narrow = pl.ds(to * HD, HD)
        rows = pl.ds(pl.multiple_of(source * PART, PART), PART)
        return [
            remote(k_in.at[:, narrow], k_loc.at[rows], prev_send.at[0, to], prev_recv.at[0, source], (after, to)),
            remote(v_in.at[:, narrow], v_loc.at[rows], prev_send.at[1, to], prev_recv.at[1, source], (after, to)),
        ]

    def forward(kv, hop, chunks):
        for chunk in chunks:
            ring_copy(kv, 0, hop, chunk).start()
            ring_copy(kv, 1, hop, chunk).start()

    for o in range(1, ROW):
        list_copy(o).start()
    loads[0].wait()
    forward(0, 1, range(CHUNKS))

    for o in range(1, ROW):
        list_copy(o).wait()
    row_lists[col] = list_in[...]
    listed = row_lists[0]
    for d in range(1, ROW):
        listed = jnp.where(device == d, row_lists[d], listed)
    plan = jnp.zeros((ROW, 128), jnp.int32)
    for rel in range(RING):
        owner = ((y + RING - rel) % RING) * ROW + col
        mine = lax.shift_right_arithmetic(listed, 4) == owner
        tile = jnp.bitwise_and(listed, HELD - 1)
        smallest = jnp.min(jnp.where(mine, tile, HELD - 1), axis=1, keepdims=True)
        largest = jnp.max(jnp.where(mine, tile, 0), axis=1, keepdims=True)
        plan = jnp.where(lane == 2 * rel, smallest, plan)
        plan = jnp.where(lane == 2 * rel + 1, largest, plan)
    table[...] = plan

    def place_own_list():
        entries = BLOCKS * SEL
        across = jnp.broadcast_to(flat[0:1], (entries, 128))
        lanes = lax.broadcasted_iota(jnp.int32, (entries, 128), 1)
        diagonal = lanes == lax.broadcasted_iota(jnp.int32, (entries, 128), 0)
        down = jnp.max(jnp.where(diagonal, across, 0), axis=1, keepdims=True)
        owner = lax.shift_right_arithmetic(down, 4)
        earlier = (lax.shift_right_arithmetic(across, 4) == owner) & (across < down)
        rank = jnp.max(jnp.where(earlier, 1, 0), axis=1, keepdims=True)
        rel = jnp.bitwise_and(y - lax.shift_right_arithmetic(owner, 3), RING - 1)
        slot = (jnp.bitwise_and(owner, ROW - 1) * RING + rel) * 2 + rank
        slot_table[...] = jnp.broadcast_to(slot, (entries, 128))

    left = lax.broadcasted_iota(jnp.int32, (TILE, HD), 1) < HALF

    def halves(lower, upper):
        turned = pltpu.roll(upper, HALF, 1)
        return jnp.where(left, lower, turned), jnp.where(left, turned, lower)

    def pack(kv, rel):
        source = blocks_of[kv][rel]

        def two(to):
            lower = source[jnp.bitwise_and(table_smem[to, 2 * rel], HELD - 1)]
            upper = source[jnp.bitwise_and(table_smem[to, 2 * rel + 1], HELD - 1)]
            return halves(lower, upper) if kv else (lower, upper)

        def one(o, carry):
            first, second = two((col + o) % ROW)
            stage[kv, rel, o - 1, 0] = first
            stage[kv, rel, o - 1, 1] = second
            return carry

        lax.fori_loop(1, ROW, one, 0, unroll=True)
        first, second = two(col)
        place = col * RING + rel
        if kv:
            got_v0[place] = first
            got_v1[place] = second
        else:
            got_k[2 * place] = first
            got_k[2 * place + 1] = second

    def hand_out(kind, rel):
        for o in range(1, ROW):
            row_copy(kind, rel, o).start()

    def hand_in(kind):
        for rel in range(RING):
            for o in range(1, ROW):
                row_copy(kind, rel, o).wait()

    def pass_on(kv, hop, chunk):
        for way in range(2):
            ring_copy(kv, way, hop, chunk).wait_recv()
            if hop < 3 or (chunk < CHUNKS // 2) == (way == 0):
                ring_copy(kv, way, hop + 1, chunk).start()

    def last_block(kv):
        for chunk in range(CHUNKS // 2):
            ring_copy(kv, 0, 4, chunk).wait_recv()
            ring_copy(kv, 1, 4, CHUNKS // 2 + chunk).wait_recv()
        pack(kv, 4)

    def block_at(step):
        return (z // 2 + step) % BLOCKS

    def gather(block, take):
        def one(j, carry):
            slot = jnp.bitwise_and(slots[block * SEL + j, 0], 2 * RING * ROW - 1)
            gathered[pl.ds(pl.multiple_of(j * TILE, TILE), TILE), :] = take(slot)
            return carry

        lax.fori_loop(0, SEL, one, 0, unroll=True)

    row = lax.broadcasted_iota(jnp.int32, (SOFT_ROWS, 2 * QB), 0)
    column = lax.broadcasted_iota(jnp.int32, (SOFT_ROWS, 2 * QB), 1)

    def score(piece, carry):
        step, head = piece // GROUP, piece % GROUP
        block = block_at(step)
        first_row = pl.multiple_of(block * QB, QB)

        @pl.when(head == 0)
        def _():
            gather(block, lambda slot: got_k[slot])
            gathered[pl.ds(REMOTE, 2 * QB), :] = k_loc[pl.ds(first_row, 2 * QB), :]

        query = q_rows[pl.ds(first_row, QB), pl.ds(pl.multiple_of(head * HD, HD), HD)]
        for pair in range(KEYS // (2 * TILE)):
            part = pl.ds(pair * 2 * TILE, 2 * TILE)
            scores[:, part] = lax.dot_general(
                query, gathered[part, :], (((1,), (1,)), ((), ())), preferred_element_type=jnp.float32
            )
        from_column = jnp.where(block + seq > 0, 0, QB)

        def soften(i, inner):
            first = pl.multiple_of(i * SOFT_ROWS, SOFT_ROWS)
            rows = pl.ds(first, SOFT_ROWS)
            kept = pl.ds(pl.multiple_of(head * QB + first, SOFT_ROWS), SOFT_ROWS)
            visible = (column - QB <= row + first) & (column >= from_column)
            far = scores[rows, pl.ds(0, REMOTE)]
            near = jnp.where(visible, scores[rows, pl.ds(REMOTE, 2 * QB)], NEG_FILL)
            top = jnp.maximum(jnp.max(far, axis=1, keepdims=True), jnp.max(near, axis=1, keepdims=True))
            far = jnp.exp2((far - top) * EXP2_SCALE)
            near = jnp.exp2((near - top) * EXP2_SCALE)
            total = jnp.sum(far, axis=1, keepdims=True) + jnp.sum(near, axis=1, keepdims=True)
            weights[step, kept, pl.ds(0, REMOTE)] = far.astype(jnp.bfloat16)
            weights[step, kept, pl.ds(REMOTE, 2 * QB)] = near.astype(jnp.bfloat16)
            inverses[step, kept, :] = jnp.broadcast_to(1.0 / total, (SOFT_ROWS, HD))
            return inner

        return lax.fori_loop(0, QB // SOFT_ROWS, soften, carry)

    place_own_list()
    copy = pltpu.make_async_copy(table, table_smem, plan_sem)
    copy.start()
    for load in loads[1:]:
        load.wait()
    copy.wait()
    pack(0, 0)
    pack(1, 0)
    hand_out(0, 0)
    pass_on(0, 1, 0)
    hand_out(1, 0)
    hand_out(2, 0)
    pass_on(0, 1, 1)
    for o in range(HEADS):
        for copy in head_copies(o):
            copy.start()

    @pl.when(is_last)
    def _():
        for to in range(HEADS):
            for copy in prior_copies(to):
                copy.start()

    pass_on(0, 1, 2)
    pass_on(0, 1, 3)
    for hop in range(1, 4):
        if hop > 1:
            for chunk in range(CHUNKS):
                pass_on(0, hop, chunk)
                if chunk == 0:
                    hand_out(0, RING - hop + 1)
        pack(0, hop)
        pack(0, RING - hop)
        hand_out(0, hop)
    forward(1, 1, range(CHUNKS))
    copy = pltpu.make_async_copy(slot_table, slots, slot_sem)
    copy.start()
    copy.wait()
    hand_out(0, 5)
    last_block(0)

    pass_on(1, 1, 0)
    hand_out(0, 4)
    for chunk in range(1, CHUNKS):
        pass_on(1, 1, chunk)
    for o in range(HEADS):
        for copy in head_copies(o):
            copy.wait()
    for source in range(2):
        rows = pl.ds(source * PART, PART)
        for kv, ref in enumerate((k_loc, v_loc)):
            pltpu.make_async_copy(ref.at[rows], ref.at[rows], prev_recv.at[kv, source]).wait()
    pack(1, 1)
    pack(1, 7)
    hand_out(1, 1)
    hand_out(2, 1)
    done = 0
    for hop in range(2, 4):
        for chunk in range(CHUNKS):
            pass_on(1, hop, chunk)
            if hop == 2 and chunk == 0:
                hand_out(1, 7)
                hand_out(2, 7)
                continue
            if hop == 2 and chunk == 1:
                hand_in(0)
            if hop == 3 and chunk == 0:
                hand_out(1, 6)
                hand_out(2, 6)
            lax.fori_loop(done, done + 2, score, 0)
            done += 2
        pack(1, hop)
        pack(1, RING - hop)
        hand_out(1, hop)
        if hop == 2:
            hand_out(2, hop)
    hand_out(1, 5)
    lax.fori_loop(done, BLOCKS * GROUP, score, 0)
    last_block(1)
    hand_out(2, 3)
    hand_out(1, 4)
    hand_out(2, 5)
    hand_out(2, 4)

    def attend(step, half):
        block = block_at(step)
        first_row = pl.multiple_of(block * QB, QB)

        def take(slot):
            on_left = jnp.bitwise_and(slot, 1) == half
            return jnp.where(left == on_left, got_v[half][lax.shift_right_logical(slot, 1)], zero)

        zero = jnp.zeros((TILE, HD), jnp.bfloat16)
        gather(block, take)
        near = v_loc[pl.ds(first_row, 2 * QB), :]
        near_left = lax.broadcasted_iota(jnp.int32, (2 * QB, HD), 1) < HALF
        gathered[pl.ds(REMOTE, 2 * QB), :] = jnp.where(near_left == (half == 0), near, jnp.zeros_like(near))
        sides = jnp.dot(weights[step], gathered[...], preferred_element_type=jnp.float32)
        result = ((sides + pltpu.roll(sides, HALF, 1)) * inverses[step]).astype(jnp.bfloat16)
        for pair in range(GROUP // 2):
            even, odd = result[2 * pair * QB : (2 * pair + 1) * QB], result[(2 * pair + 1) * QB : (2 * pair + 2) * QB]
            out_stage[half, pl.ds(first_row, QB), pl.ds(pair * HD, HD)] = jnp.where(left, even, odd)

    def return_copy(step, half, to, place):
        rows = pl.ds(pl.multiple_of(to * PART, PART), PART)
        part = pl.ds(pl.multiple_of(z * (WIDE // 2), WIDE // 2), WIDE // 2)
        src, dst = out_stage.at[half, rows], out_parts.at[half, :, part]
        if place is None:
            return pltpu.make_async_copy(src, dst, o_local.at[half])
        return remote(src, dst, o_send.at[half, place], o_recv.at[half, place], (seq, to))

    returns = []
    for half in range(2):
        hand_in(1 + half)
        for step in ORDER:
            attend(step, half)
            if step != 0:
                for parity in range(2):
                    to = 2 * block_at(step) + parity
                    returns.append(return_copy(step, half, to, 2 * step + (z + parity) % 2))
            else:
                returns.append(return_copy(step, half, z + 1 - 2 * (z % 2), 0))
                returns.append(return_copy(step, half, z, None))
            returns[-2].start()
            returns[-1].start()
    for copy in returns:
        copy.wait()

    part_left = lax.broadcasted_iota(jnp.int32, (PART, HD), 1) < HALF
    for pair in range(HEADS * GROUP // 2):
        lanes = pl.ds(pair * HD, HD)
        first, second = out_parts[0, :, lanes], out_parts[1, :, lanes]
        out[:, pl.ds(2 * pair * HD, HD)] = jnp.where(part_left, first, pltpu.roll(second, HALF, 1))
        out[:, pl.ds((2 * pair + 1) * HD, HD)] = jnp.where(part_left, pltpu.roll(first, HALF, 1), second)

    for kv in range(2):
        for hop in range(1, 5):
            for chunk in range(CHUNKS):
                for way in range(2):
                    if hop < 4 or (chunk < CHUNKS // 2) == (way == 0):
                        ring_copy(kv, way, hop, chunk).wait_send()

    @pl.when(is_last)
    def _():
        for to in range(HEADS):
            for copy in prior_copies(to):
                copy.wait_send()


def on_device(queries, new_keys, new_values, cache_keys, cache_values, tile_lists):
    tiles = pltpu.VMEM((HELD, TILE, HD), jnp.bfloat16)
    dma = pltpu.SemaphoreType.DMA
    vmem = pl.BlockSpec(memory_space=pltpu.VMEM)
    return pl.pallas_call(
        kernel,
        out_shape=pltpu.VMEM((PART, HEADS * WIDE), jnp.bfloat16),
        in_specs=[pl.BlockSpec(memory_space=pl.ANY)] * 5 + [vmem],
        out_specs=vmem,
        scratch_shapes=[
            pltpu.VMEM((PART, HEADS * WIDE), jnp.bfloat16),
            pltpu.VMEM((PART, HEADS * HD), jnp.bfloat16),
            pltpu.VMEM((PART, HEADS * HD), jnp.bfloat16),
            tiles,
            tiles,
            pltpu.VMEM((ROWS, WIDE), jnp.bfloat16),
            pltpu.VMEM((QB + ROWS, HD), jnp.bfloat16),
            pltpu.VMEM((QB + ROWS, HD), jnp.bfloat16),
            pltpu.VMEM((8, 128), jnp.int32),
            pltpu.VMEM((8, 128), jnp.int32),
            pltpu.VMEM((ROW, 8, 128), jnp.int32),
            pltpu.VMEM((ROW, 128), jnp.int32),
            pltpu.SMEM((ROW, 128), jnp.int32),
            pltpu.VMEM((BLOCKS * SEL, 128), jnp.int32),
            pltpu.SMEM((BLOCKS * SEL, 128), jnp.int32),
            *([tiles] * 14),
            pltpu.VMEM((2, RING, ROW - 1, 2, TILE, HD), jnp.bfloat16),
            pltpu.VMEM((2 * RING * ROW, TILE, HD), jnp.bfloat16),
            pltpu.VMEM((RING * ROW, TILE, HD), jnp.bfloat16),
            pltpu.VMEM((RING * ROW, TILE, HD), jnp.bfloat16),
            pltpu.VMEM((KEYS, HD), jnp.bfloat16),
            pltpu.VMEM((QB, KEYS), jnp.float32),
            pltpu.VMEM((BLOCKS, GROUP * QB, KEYS), jnp.bfloat16),
            pltpu.VMEM((BLOCKS, GROUP * QB, HD), jnp.float32),
            pltpu.VMEM((2, ROWS, WIDE // 2), jnp.bfloat16),
            pltpu.VMEM((2, PART, HEADS * WIDE // 2), jnp.bfloat16),
            dma((5,)),
            dma((ROW - 1,)),
            dma((ROW - 1,)),
            dma,
            dma,
            dma((2, 2, 4, CHUNKS)),
            dma((2, 2, 4, CHUNKS)),
            dma((3, RING, ROW - 1)),
            dma((3, RING, ROW - 1)),
            dma((3, HEADS - 1)),
            dma((3, HEADS - 1)),
            dma((3,)),
            dma((2, HEADS)),
            dma((2, 2)),
            dma((2, HEADS)),
            dma((2, HEADS)),
            dma((2,)),
        ],
        compiler_params=pltpu.CompilerParams(
            collective_id=0, has_side_effects=True, vmem_limit_bytes=64000 * 1024
        ),
    )(
        queries,
        new_keys,
        new_values,
        cache_keys.reshape(HELD, TILE, HD),
        cache_values.reshape(HELD, TILE, HD),
        tile_lists,
    )


def solution(mesh):
    return jax.shard_map(
        on_device,
        mesh=mesh,
        in_specs=(
            P(("seq", "head"), None),
            P(("seq", "head"), None),
            P(("seq", "head"), None),
            P("seq", "head"),
            P("seq", "head"),
            P("seq", "head", None),
        ),
        out_specs=P(("seq", "head"), None),
        check_vma=False,
    )
```
